512 devices in a mesh: lon: 8 (over y_lo, core), lat: 64 (over x, y_hi, z).
Axes of the slice: x: 4, y: 8 (y_hi: 2, y_lo: 4; y = y_hi * 4 + y_lo), z: 8, core: 2. Of those that a mesh axis runs over, the one named last changes fastest.
Arguments:
- ocean_state: bfloat16 [1, 384, 512, 256], P(None, 'lat', 'lon'), may hold values from -6 to 6
- land_sea: int32 [1, 384, 512], P(None, 'lat', 'lon'), may hold values 0 or 1
- cotangent: bfloat16 [1, 384, 512, 256], P(None, 'lat', 'lon'), may hold values from -6 to 6
- dw_kernel: float32 [7, 7, 256], replicated, may hold values from -0.875 to 0.875
- dw_bias: float32 [256], replicated, may hold values from -3 to 3
- ln_gain: float32 [256], replicated, may hold values from 0.1 to 1.9
- ln_bias: float32 [256], replicated, may hold values from -2 to 2
- w_in: bfloat16 [256, 1024], replicated, may hold values from -0.375 to 0.375
- b_in: float32 [1024], replicated, may hold values from -2 to 2
- w_out: bfloat16 [1024, 256], replicated, may hold values from -0.1875 to 0.1875
- b_out: float32 [256], replicated, may hold values from -2 to 2
- layer_scale: float32 [256], replicated, may hold values from 0.3 to 1.5
Outputs:
- output: bfloat16 [1, 384, 512, 256], P(None, 'lat', 'lon')
- grad_state: bfloat16 [1, 384, 512, 256], P(None, 'lat', 'lon')
- grad_kernel: float32 [7, 7, 256], replicated
- grad_dw_bias: float32 [256], replicated
- grad_ln_gain: float32 [256], replicated
- grad_ln_bias: float32 [256], replicated
- grad_w_in: float32 [256, 1024], replicated
- grad_b_in: float32 [1024], replicated
- grad_w_out: float32 [1024, 256], replicated
- grad_b_out: float32 [256], replicated
- grad_scale: float32 [256], replicated
The draws below stay inside these ranges and needn't reach their ends.
All inputs are finite; a program needn't handle non-finite values. No bound on the sum of `land_sea` on one device may be relied on, other than what follows from the above.
Results may differ from the reference program's by a relative error of at most 0.0085.
Values may be sent and summed in bfloat16 or wider, within the bound.
No kernel may reach another device: no remote copies, remote signals or barrier semaphores. Data moves between devices by JAX's collectives and lax.ppermute only.
A program may use at most 64 MiB of HBM per device.

```python
import math
import jax
import jax.numpy as jnp
from jax import lax

C = 256
HID = 1024
BATCH = 1
LAT = 384
LON = 512


def place_ends(result, stream_key, smallest, high):
    shape = result.shape
    place = [jax.random.randint(jax.random.fold_in(stream_key, axis), (), 0, shape[axis]) for axis in range(len(shape))]
    result = result.at[tuple(place)].set(smallest)
    longest = shape.index(max(shape))
    place[longest] = (place[longest] + 1) % shape[longest]
    return result.at[tuple(place)].set(high)


def levels(own_key, shape, split, low, top_value):
    factor_of = 1.0
    for dim, shards_of in split:
        steps = jax.random.uniform(jax.random.fold_in(jax.random.fold_in(own_key, 6), dim), (shards_of,), jnp.float32, low / len(split), top_value / len(split))
        factor_of = factor_of * jnp.repeat(jnp.exp(steps), shape[dim] // shards_of).reshape((-1,) + (1,) * (len(shape) - 1 - dim))
    return factor_of


def bell_draw(key, shape, deviation, limit, shards=(), dtype=jnp.bfloat16):
    drawn = jax.random.normal(key, shape, jnp.float32) * deviation
    if len(shards) > 0:
        drawn = levels(key, shape, shards, -0.22, 0.18) * drawn
    return jnp.clip(drawn, min=-limit, max=limit).astype(dtype)


def setup_inputs(seed: int = 0) -> dict:
    splits = jax.random.split(jax.random.key(seed), 13)
    ocean_state = bell_draw(splits[0], (BATCH, LAT, LON, C), 1.0, 6.0, ((1, 64), (2, 8)))
    land_sea = place_ends((jax.random.randint(splits[1], (BATCH, LAT, LON), 0, 3) < 2).astype(jnp.int32), jax.random.fold_in(splits[1], 1), 0, 1)
    cotangent = bell_draw(splits[2], (BATCH, LAT, LON, C), 1.0, 6.0, ((1, 64), (2, 8)))
    dw_kernel = bell_draw(splits[3], (7, 7, C), 49 ** -0.5, 0.875, (), jnp.float32)
    dw_bias = bell_draw(splits[4], (C,), 0.5, 3.0, (), jnp.float32)
    ln_gain = jnp.clip(1.0 + 0.18 * jax.random.normal(splits[5], (C,), jnp.float32), 0.1, 1.9)
    ln_bias = bell_draw(splits[6], (C,), 0.3, 2.0, (), jnp.float32)
    w_in = bell_draw(splits[7], (C, HID), C ** -0.5, 0.375)
    b_in = bell_draw(splits[8], (HID,), 0.3, 2.0, (), jnp.float32)
    w_out = bell_draw(splits[9], (HID, C), HID ** -0.5, 0.1875)
    b_out = bell_draw(splits[10], (C,), 0.3, 2.0, (), jnp.float32)
    layer_scale = jnp.clip(jnp.exp(jax.random.uniform(splits[11], (C,), jnp.float32, math.log(0.3), math.log(1.5))), 0.3, 1.5)
    return {"ocean_state": ocean_state, "land_sea": land_sea, "cotangent": cotangent, "dw_kernel": dw_kernel, "dw_bias": dw_bias, "ln_gain": ln_gain, "ln_bias": ln_bias, "w_in": w_in, "b_in": b_in, "w_out": w_out, "b_out": b_out, "layer_scale": layer_scale}


def depthwise(padded, kernel, num_rows, num_cols):
    summed = jnp.zeros((padded.shape[0], num_rows, num_cols, padded.shape[3]), jnp.float32)
    for row_off in range(7):
        for col_off in range(7):
            summed = summed + padded[:, row_off:row_off + num_rows, col_off:col_off + num_cols, :].astype(jnp.float32) * kernel[row_off, col_off]
    return summed

def transposed(padded, kernel, num_rows, num_cols):
    summed = jnp.zeros((padded.shape[0], num_rows, num_cols, padded.shape[3]), jnp.float32)
    for row_off in range(7):
        for col_off in range(7):
            summed = summed + padded[:, 6 - row_off:6 - row_off + num_rows, 6 - col_off:6 - col_off + num_cols, :].astype(jnp.float32) * kernel[row_off, col_off]
    return summed

def kernel_terms(padded, grad_depth, num_rows, num_cols):
    grad_float = grad_depth.astype(jnp.float32)
    rows_out = []
    for row_off in range(7):
        cols_out = []
        for col_off in range(7):
            window = padded[:, row_off:row_off + num_rows, col_off:col_off + num_cols, :].astype(jnp.float32)
            cols_out.append(lax.optimization_barrier(jnp.sum(window * grad_float, axis=(0, 1, 2))))
        rows_out.append(jnp.stack(cols_out))
    return jnp.stack(rows_out)

def forward_tokens(depth_out, ln_gain, ln_bias, w_in, b_in, w_out, b_out):
    center = depth_out - lax.optimization_barrier(jnp.mean(depth_out, axis=-1, keepdims=True))
    inv_std = lax.rsqrt(lax.optimization_barrier(jnp.mean(center * center, axis=-1, keepdims=True)) + 1e-06)
    norm_hat = center * inv_std
    normed = (norm_hat * ln_gain + ln_bias).astype(jnp.bfloat16)
    pre_act = jnp.dot(normed, w_in, preferred_element_type=jnp.float32) + b_in
    activated = jax.nn.gelu(pre_act, approximate=True).astype(jnp.bfloat16)
    branch = jnp.dot(activated, w_out, preferred_element_type=jnp.float32) + b_out
    return (norm_hat, inv_std, normed, pre_act, activated, branch)

def backward_tokens(masked, norm_hat, inv_std, pre_act, ln_gain, w_in, w_out, layer_scale):
    grad_branch = (masked * layer_scale).astype(jnp.bfloat16)
    grad_act = lax.dot_general(grad_branch, w_out, (((1,), (1,)), ((), ())), preferred_element_type=jnp.float32)
    unused, pull_back = jax.vjp(lambda v: jax.nn.gelu(v, approximate=True), pre_act)
    grad_pre = pull_back(grad_act)[0].astype(jnp.bfloat16)
    grad_norm = lax.dot_general(grad_pre, w_in, (((1,), (1,)), ((), ())), preferred_element_type=jnp.float32)
    scaled = grad_norm * ln_gain
    grad_depth = (inv_std * (scaled - lax.optimization_barrier(jnp.mean(scaled, axis=-1, keepdims=True)) - norm_hat * lax.optimization_barrier(jnp.mean(scaled * norm_hat, axis=-1, keepdims=True)))).astype(jnp.bfloat16)
    return (grad_branch, grad_pre, grad_norm, grad_depth)

def weight_terms(masked, branch, grad_branch, activated, normed, grad_pre, grad_norm, norm_hat):
    dims = (((0,), (0,)), ((), ()))
    grad_w_in = lax.dot_general(normed, grad_pre, dims, preferred_element_type=jnp.float32)
    grad_w_out = lax.dot_general(activated, grad_branch, dims, preferred_element_type=jnp.float32)
    return (grad_w_in, grad_w_out, lax.optimization_barrier(jnp.sum(grad_pre.astype(jnp.float32), axis=0)), lax.optimization_barrier(jnp.sum(grad_branch.astype(jnp.float32), axis=0)), lax.optimization_barrier(jnp.sum(masked * branch, axis=0)), lax.optimization_barrier(jnp.sum(grad_norm * norm_hat, axis=0)), lax.optimization_barrier(jnp.sum(grad_norm, axis=0)))

def rim_pad(field):
    lon_ext = jnp.concatenate([field[:, :, -3:], field, field[:, :, :3]], axis=2)
    return jnp.pad(lon_ext, ((0, 0), (3, 3), (0, 0), (0, 0)))

def reference(ocean_state, land_sea, cotangent, dw_kernel, dw_bias, ln_gain, ln_bias, w_in, b_in, w_out, b_out, layer_scale):
    num_batch, num_rows, num_cols, channels = ocean_state.shape
    padded = rim_pad(ocean_state)
    depth_out = depthwise(padded, dw_kernel, num_rows, num_cols) + dw_bias
    mask_float = land_sea.astype(jnp.float32)[..., None]
    masked = mask_float * cotangent.astype(jnp.float32)
    depth_rows = depth_out.reshape(num_batch * num_rows, num_cols, channels)
    masked_rows = masked.reshape(num_batch * num_rows, num_cols, channels)
    hidden = w_in.shape[1]
    start = (jnp.zeros((channels, hidden), jnp.float32), jnp.zeros((hidden, channels), jnp.float32), jnp.zeros((hidden,), jnp.float32), jnp.zeros((channels,), jnp.float32), jnp.zeros((channels,), jnp.float32), jnp.zeros((channels,), jnp.float32), jnp.zeros((channels,), jnp.float32))

    def one_row(running, pieces):
        depth_row, masked_row = pieces
        norm_hat, inv_std, normed, pre_act, activated, branch = forward_tokens(depth_row, ln_gain, ln_bias, w_in, b_in, w_out, b_out)
        grad_branch, grad_pre, grad_norm, grad_depth = backward_tokens(masked_row, norm_hat, inv_std, pre_act, ln_gain, w_in, w_out, layer_scale)
        fresh = weight_terms(masked_row, branch, grad_branch, activated, normed, grad_pre, grad_norm, norm_hat)
        return (jax.tree.map(lambda a, b: a + b, running, fresh), (branch, grad_depth))
    totals, (branch_rows, grad_rows) = lax.scan(one_row, start, (depth_rows, masked_rows))
    branch = branch_rows.reshape(num_batch, num_rows, num_cols, channels)
    grad_depth = grad_rows.reshape(num_batch, num_rows, num_cols, channels)
    output = (ocean_state.astype(jnp.float32) + mask_float * layer_scale * branch).astype(jnp.bfloat16)
    grad_pad = rim_pad(grad_depth)
    grad_state = (cotangent.astype(jnp.float32) + transposed(grad_pad, dw_kernel, num_rows, num_cols)).astype(jnp.bfloat16)
    factor = 1.0 / jnp.sqrt(jnp.float32(num_batch * num_rows * num_cols))
    grad_kernel = kernel_terms(padded, grad_depth, num_rows, num_cols) * factor
    grad_dw_bias = lax.optimization_barrier(jnp.sum(grad_depth.astype(jnp.float32), axis=(0, 1, 2))) * factor
    grad_w_in, grad_w_out, grad_b_in, grad_b_out, grad_scale, grad_ln_gain, grad_ln_bias = totals
    return (output, grad_state, grad_kernel, grad_dw_bias, grad_ln_gain * factor, grad_ln_bias * factor, grad_w_in * factor, grad_b_in * factor, grad_w_out * factor, grad_b_out * factor, grad_scale * factor)
```

```python
import jax
import jax.numpy as jnp
import numpy as np
from jax import lax
from jax.sharding import Mesh, PartitionSpec as P

LON = ("y_lo", "core")
LAT = ("x", "y_hi", "z")
FAR = ("x", "y_hi", "y_lo", "z")


def whole_sum(chunks):
    far = lax.axis_size(FAR)
    pair = chunks.astype(jnp.bfloat16).reshape(2, far * 5, 256)
    pair = lax.all_to_all(pair, "core", 0, 0)
    value = (pair[0].astype(jnp.float32) + pair[1].astype(jnp.float32)).astype(jnp.bfloat16)
    value = lax.all_to_all(value.reshape(far, 2, 640), FAR, 0, 0)
    value = jnp.sum(value.astype(jnp.float32), axis=0).astype(jnp.bfloat16)
    value = lax.all_to_all(jnp.broadcast_to(value[None], (far, 2, 640)), FAR, 0, 0)
    mine = value.reshape(far, 5, 256)
    other = lax.ppermute(mine, "core", [(0, 1), (1, 0)])
    is_first = lax.axis_index("core") == 0
    return jnp.where(is_first, mine, other), jnp.where(is_first, other, mine)


def extended(array, sides, width, wrap):
    for axis, dim in sides:
        size, length = (lax.axis_size(axis), array.shape[dim])
        up = [(i, (i + 1) % size) for i in range(size if wrap else size - 1)]
        down = [(j, i) for i, j in up]
        last = lax.slice_in_dim(array, length - width, length, axis=dim)
        leading = lax.slice_in_dim(array, 0, width, axis=dim)
        before = lax.ppermute(last, axis, up)
        after = lax.ppermute(leading, axis, down)
        array = jnp.concatenate([before, array, after], axis=dim)
    return array


def depthwise(padded, kernel, num_rows, num_cols):
    summed = jnp.zeros((padded.shape[0], num_rows, num_cols, padded.shape[3]), jnp.float32)
    for row_off in range(7):
        for col_off in range(7):
            summed = (
                summed
                + padded[:, row_off : row_off + num_rows, col_off : col_off + num_cols, :].astype(
                    jnp.float32
                )
                * kernel[row_off, col_off]
            )
    return summed


def transposed(padded, kernel, num_rows, num_cols):
    summed = jnp.zeros((padded.shape[0], num_rows, num_cols, padded.shape[3]), jnp.float32)
    for row_off in range(7):
        for col_off in range(7):
            summed = (
                summed
                + padded[
                    :, 6 - row_off : 6 - row_off + num_rows, 6 - col_off : 6 - col_off + num_cols, :
                ].astype(jnp.float32)
                * kernel[row_off, col_off]
            )
    return summed


def kernel_terms(padded, grad_depth, num_rows, num_cols):
    grad_float = grad_depth.astype(jnp.float32)
    rows_out = []
    for row_off in range(7):
        cols_out = []
        for col_off in range(7):
            window = padded[
                :, row_off : row_off + num_rows, col_off : col_off + num_cols, :
            ].astype(jnp.float32)
            cols_out.append(jnp.sum(window * grad_float, axis=(0, 1, 2)))
        rows_out.append(jnp.stack(cols_out))
    return jnp.stack(rows_out)


def forward_tokens(depth_out, ln_gain, ln_bias, w_in, b_in, w_out, b_out):
    center = depth_out - jnp.mean(depth_out, axis=-1, keepdims=True)
    inv_std = lax.rsqrt(jnp.mean(center * center, axis=-1, keepdims=True) + 1e-06)
    norm_hat = center * inv_std
    normed = (norm_hat * ln_gain + ln_bias).astype(jnp.bfloat16)
    pre_act = jnp.dot(normed, w_in, preferred_element_type=jnp.float32) + b_in
    activated = jax.nn.gelu(pre_act, approximate=True).astype(jnp.bfloat16)
    branch = jnp.dot(activated, w_out, preferred_element_type=jnp.float32) + b_out
    return (norm_hat, inv_std, normed, pre_act, activated, branch)


def backward_tokens(masked, norm_hat, inv_std, pre_act, ln_gain, w_in, w_out, layer_scale):
    grad_branch = (masked * layer_scale).astype(jnp.bfloat16)
    grad_act = lax.dot_general(
        grad_branch, w_out, (((1,), (1,)), ((), ())), preferred_element_type=jnp.float32
    )
    unused, pull_back = jax.vjp(lambda v: jax.nn.gelu(v, approximate=True), pre_act)
    grad_pre = pull_back(grad_act)[0].astype(jnp.bfloat16)
    grad_norm = lax.dot_general(
        grad_pre, w_in, (((1,), (1,)), ((), ())), preferred_element_type=jnp.float32
    )
    scaled = grad_norm * ln_gain
    grad_depth = (
        inv_std
        * (
            scaled
            - jnp.mean(scaled, axis=-1, keepdims=True)
            - norm_hat * jnp.mean(scaled * norm_hat, axis=-1, keepdims=True)
        )
    ).astype(jnp.bfloat16)
    return (grad_branch, grad_pre, grad_norm, grad_depth)


def weight_terms(masked, branch, grad_branch, activated, normed, grad_pre, grad_norm, norm_hat):
    dims = (((0,), (0,)), ((), ()))
    grad_w_in = lax.dot_general(normed, grad_pre, dims, preferred_element_type=jnp.float32)
    grad_w_out = lax.dot_general(activated, grad_branch, dims, preferred_element_type=jnp.float32)
    return (
        grad_w_in,
        grad_w_out,
        jnp.sum(grad_pre.astype(jnp.float32), axis=0),
        jnp.sum(grad_branch.astype(jnp.float32), axis=0),
        jnp.sum(masked * branch, axis=0),
        jnp.sum(grad_norm * norm_hat, axis=0),
        jnp.sum(grad_norm, axis=0),
    )


def local(
    ocean_state,
    land_sea,
    cotangent,
    dw_kernel,
    dw_bias,
    ln_gain,
    ln_bias,
    w_in,
    b_in,
    w_out,
    b_out,
    layer_scale,
):
    num_batch, num_rows, num_cols, channels = ocean_state.shape
    mask_float = land_sea.astype(jnp.float32)[..., None]
    lon_ext = extended(ocean_state, ((LON, 2),), 3, True)
    padded = extended(lon_ext, ((LAT, 1),), 3, False)
    depth_out = depthwise(padded, dw_kernel, num_rows, num_cols) + dw_bias
    masked = (mask_float * cotangent.astype(jnp.float32)).reshape(-1, channels)
    norm_hat, inv_std, normed, pre_act, activated, branch = forward_tokens(
        depth_out.reshape(-1, channels), ln_gain, ln_bias, w_in, b_in, w_out, b_out
    )
    grad_branch, grad_pre, grad_norm, grad_flat = backward_tokens(
        masked, norm_hat, inv_std, pre_act, ln_gain, w_in, w_out, layer_scale
    )
    grad_terms = weight_terms(
        masked, branch, grad_branch, activated, normed, grad_pre, grad_norm, norm_hat
    )
    grad_depth = grad_flat.reshape(num_batch, num_rows, num_cols, channels)
    grad_ext = extended(grad_depth, ((LON, 2),), 3, True)
    grad_pad = extended(grad_ext, ((LAT, 1),), 3, False)
    branch_own = branch.reshape(num_batch, num_rows, num_cols, channels)
    output = (ocean_state.astype(jnp.float32) + mask_float * layer_scale * branch_own).astype(
        jnp.bfloat16
    )
    grad_state = (
        cotangent.astype(jnp.float32) + transposed(grad_pad, dw_kernel, num_rows, num_cols)
    ).astype(jnp.bfloat16)
    kernel_part = kernel_terms(padded, grad_depth, num_rows, num_cols)
    bias_part = jnp.sum(grad_depth.astype(jnp.float32), axis=(0, 1, 2))
    grad_w_in, grad_w_out, grad_b_in, grad_b_out, grad_scale, grad_ln_gain, grad_ln_bias = (
        grad_terms
    )
    all_cells = num_batch * num_rows * num_cols * lax.axis_size(LON) * lax.axis_size(LAT)
    factor = 1.0 / jnp.sqrt(jnp.float32(all_cells))
    hidden = w_in.shape[1]
    blocks = hidden // channels
    smalls = (
        kernel_part.reshape(-1, channels),
        grad_b_in.reshape(-1, channels),
        bias_part[None],
        grad_ln_gain[None],
        grad_ln_bias[None],
        grad_b_out[None],
        grad_scale[None],
    )
    parts = [grad_w_in[:, k * channels : (k + 1) * channels] for k in range(blocks)]
    big_terms = jnp.concatenate(parts + [grad_w_out]).reshape(-1, 4, channels)
    small_terms = jnp.concatenate(smalls)
    spare = big_terms.shape[0] - small_terms.shape[0]
    small_terms = jnp.pad(small_terms, ((0, spare), (0, 0)))[:, None]
    first, second = whole_sum(jnp.concatenate([big_terms, small_terms], axis=1))
    total = first[:, :4].reshape(hidden, channels).astype(jnp.float32) * factor
    grad_w_in = jnp.concatenate(
        [total[k * channels : (k + 1) * channels] for k in range(blocks)], axis=1
    )
    grad_w_out = second[:, :4].reshape(hidden, channels).astype(jnp.float32) * factor
    total = first[:, 4].astype(jnp.float32) * factor
    kernel_part = total[:49].reshape(7, 7, channels)
    at = 49
    grad_b_in = total[at : at + blocks].reshape(hidden)
    at += blocks
    return (
        output,
        grad_state,
        kernel_part,
        total[at],
        total[at + 1],
        total[at + 2],
        grad_w_in,
        grad_b_in,
        grad_w_out,
        total[at + 3],
        total[at + 4],
    )


def solution(mesh):
    devices = mesh.devices.reshape(4, 2, 4, 2, 8)
    mesh = Mesh(devices, ("y_lo", "core", "x", "y_hi", "z"))
    in_specs = (
        P(None, LAT, LON, None),
        P(None, LAT, LON),
        P(None, LAT, LON, None),
        P(),
        P(),
        P(),
        P(),
        P(),
        P(),
        P(),
        P(),
        P(),
    )
    out_specs = (
        P(None, LAT, LON, None),
        P(None, LAT, LON, None),
        P(),
        P(),
        P(),
        P(),
        P(),
        P(),
        P(),
        P(),
        P(),
    )
    return jax.shard_map(local, mesh=mesh, in_specs=in_specs, out_specs=out_specs, check_vma=False)
```

```python
import functools
import math

import jax
import jax.numpy as jnp
from jax import lax
from jax.experimental import pallas as pl
from jax.experimental.pallas import tpu as pltpu
from jax.sharding import Mesh, PartitionSpec as P

LON = ("y_lo", "core")
LAT = ("x", "y_hi", "z")
FAR = ("x", "y_hi", "y_lo", "z")
LANES = 128
VMEM_BYTES = 44 << 20
F32 = jnp.float32
BF16 = jnp.bfloat16


def dot(a, b, ca, cb):
    return lax.dot_general(a, b, (((ca,), (cb,)), ((), ())), preferred_element_type=F32)


def fill_padded(pad_ref, own_ref, up_ref, down_ref, left_ref, right_ref, top_ref, low_ref):
    rows, cols, _ = own_ref.shape
    for t in range(2):
        ln = slice(t * LANES, (t + 1) * LANES)
        pad_ref[t, 0:3, 8 : 8 + cols] = up_ref[:, :, ln].astype(F32)
        pad_ref[t, 3 : 3 + rows, 8 : 8 + cols] = own_ref[:, :, ln].astype(F32)
        pad_ref[t, 3 + rows : 6 + rows, 8 : 8 + cols] = down_ref[:, :, ln].astype(F32)
        pad_ref[t, 3 : 3 + rows, 5:8] = left_ref[:, :, ln].astype(F32)
        pad_ref[t, 3 : 3 + rows, 8 + cols : 11 + cols] = right_ref[:, :, ln].astype(F32)
        pad_ref[t, 0:3, 5:8] = top_ref[:, 0:3, ln].astype(F32)
        pad_ref[t, 0:3, 8 + cols : 11 + cols] = top_ref[:, 3:6, ln].astype(F32)
        pad_ref[t, 3 + rows : 6 + rows, 5:8] = low_ref[:, 0:3, ln].astype(F32)
        pad_ref[t, 3 + rows : 6 + rows, 8 + cols : 11 + cols] = low_ref[:, 3:6, ln].astype(F32)


def convolve(pad_ref, k_ref, out_ref, rows, cols, flip):
    blocks = cols // 8

    def step(n, carry):
        t = n // blocks
        at = pl.multiple_of((n % blocks) * 8, 8)
        acc = [jnp.zeros((8, LANES), F32) for _ in range(rows)]
        for j in range(7):
            window = [pad_ref[t, r, pl.ds(at + 5 + j, 8), :] for r in range(rows + 6)]
            for i in range(7):
                tap = (6 - i) * 7 + 6 - j if flip else i * 7 + j
                weight = k_ref[t, tap : tap + 1, :]
                for p in range(rows):
                    acc[p] = acc[p] + window[p + i] * weight
        for p in range(rows):
            out_ref[t, p, pl.ds(at, 8), :] = acc[p]
        return carry

    lax.fori_loop(0, 2 * blocks, step, 0)


def kernel_sums(pad_ref, grad_ref, out_ref, rows, cols):
    def step(n, carry):
        t, j = n // 7, n % 7
        acc = [jnp.zeros((8, LANES), F32) for _ in range(7)]
        for b in range(cols // 8):
            window = [pad_ref[t, r, pl.ds(b * 8 + 5 + j, 8), :] for r in range(rows + 6)]
            grad = [grad_ref[t, p, b * 8 : b * 8 + 8, :] for p in range(rows)]
            for i in range(7):
                for p in range(rows):
                    acc[i] = acc[i] + window[p + i] * grad[p]
        for i in range(7):
            out_ref[t, j, i] = acc[i]
        return carry

    lax.fori_loop(0, 14, step, 0)


def block_kernel(
    own_ref, up_ref, down_ref, left_ref, right_ref, top_ref, low_ref, mask_ref, masked_ref, k_ref, dw_bias_ref,
    gain_ref, bias_ref, w_in_ref, b_in_ref, w_out_ref, b_out_ref, scale_ref,
    out_ref, grad_ref, big_ref, small_ref,
    pad_ref, depth_ref, terms_ref,
):
    rows, cols, channels = own_ref.shape
    cells = rows * cols
    hidden = w_in_ref.shape[1]
    halves = channels // LANES
    fill_padded(pad_ref, own_ref, up_ref, down_ref, left_ref, right_ref, top_ref, low_ref)
    convolve(pad_ref, k_ref, depth_ref, rows, cols, False)
    depth = jnp.concatenate([depth_ref[t].reshape(cells, LANES) for t in range(2)], axis=1)
    depth = depth + dw_bias_ref[...]
    center = depth - jnp.mean(depth, axis=-1, keepdims=True)
    inv_std = lax.rsqrt(jnp.mean(center * center, axis=-1, keepdims=True) + 1e-6)
    norm_hat = center * inv_std
    normed = (norm_hat * gain_ref[...] + bias_ref[...]).astype(BF16)
    masked = masked_ref[...].astype(F32)
    grad_branch = (masked * scale_ref[...]).astype(BF16)
    branch = jnp.zeros((cells, channels), F32)
    grad_norm = jnp.zeros((cells, channels), F32)
    root = math.sqrt(2.0 / math.pi)
    b_in_sums = []
    width = channels
    for h in range(hidden // width):
        at = slice(h * width, (h + 1) * width)
        w_in = w_in_ref[:, at]
        w_out = w_out_ref[at, :]
        pre = dot(normed, w_in, 1, 0) + b_in_ref[:, at]
        square = pre * pre
        bent = jnp.tanh(root * pre * (1.0 + 0.044715 * square))
        half = 0.5 * (1.0 + bent)
        act = (pre * half).astype(BF16)
        slope = half + (0.5 * root) * pre * (1.0 - bent * bent) * (1.0 + (3 * 0.044715) * square)
        grad_pre = (dot(grad_branch, w_out, 1, 1) * slope).astype(BF16)
        branch = branch + dot(act, w_out, 1, 0)
        grad_norm = grad_norm + dot(grad_pre, w_in, 1, 1)
        g_in = dot(normed, grad_pre, 0, 0).astype(BF16)
        g_out = dot(act, grad_branch, 0, 0).astype(BF16)
        for t in range(width // LANES):
            base = (h * (width // LANES) + t) * channels
            big_ref[base : base + channels, :] = g_in[:, t * LANES : (t + 1) * LANES]
        for t in range(halves):
            base = hidden * halves + t * hidden + h * width
            big_ref[base : base + width, :] = g_out[:, t * LANES : (t + 1) * LANES]
        b_in_sums.append(jnp.sum(grad_pre.astype(F32), axis=0, keepdims=True))
    branch = branch + b_out_ref[...]
    mask = mask_ref[...].astype(F32)
    own = own_ref[...].reshape(cells, channels).astype(F32)
    out_ref[...] = (own + mask * scale_ref[...] * branch).astype(BF16).reshape(rows, cols, channels)
    scaled = grad_norm * gain_ref[...]
    mean_u = jnp.mean(scaled, axis=-1, keepdims=True)
    mean_un = jnp.mean(scaled * norm_hat, axis=-1, keepdims=True)
    grad_depth = (inv_std * (scaled - mean_u - norm_hat * mean_un)).astype(BF16)
    grad_ref[...] = grad_depth.reshape(rows, cols, channels)
    grad_float = grad_depth.astype(F32)
    for t in range(2):
        depth_ref[t] = grad_float[:, t * LANES : (t + 1) * LANES].reshape(rows, cols, LANES)
    kernel_sums(pad_ref, depth_ref, terms_ref, rows, cols)
    singles = b_in_sums + [
        jnp.sum(grad_float, axis=0, keepdims=True),
        jnp.sum(grad_norm * norm_hat, axis=0, keepdims=True),
        jnp.sum(grad_norm, axis=0, keepdims=True),
        jnp.sum(grad_branch.astype(F32), axis=0, keepdims=True),
        jnp.sum(masked * branch, axis=0, keepdims=True),
    ]
    for t in range(2):
        ln = slice(t * LANES, (t + 1) * LANES)
        small_ref[t, 0:49, :] = jnp.sum(terms_ref[t].reshape(49, 8, LANES), axis=1)
        for n, single in enumerate(singles):
            small_ref[t, 49 + n : 50 + n, :] = single[:, ln]
        small_ref[t, 49 + len(singles) :, :] = jnp.zeros((64 - 49 - len(singles), LANES), F32)


def state_kernel(
    own_ref, up_ref, down_ref, left_ref, right_ref, top_ref, low_ref, cot_ref, k_ref, out_ref, pad_ref, sum_ref
):
    rows, cols, _ = own_ref.shape
    fill_padded(pad_ref, own_ref, up_ref, down_ref, left_ref, right_ref, top_ref, low_ref)
    convolve(pad_ref, k_ref, sum_ref, rows, cols, True)
    for t in range(2):
        ln = slice(t * LANES, (t + 1) * LANES)
        out_ref[:, :, ln] = (cot_ref[:, :, ln].astype(F32) + sum_ref[t]).astype(BF16)


def unpack_kernel(factor, core_ref, mine_ref, other_ref, w_in_ref, w_out_ref):
    channels, hidden = w_in_ref.shape

    def write(first_ref, second_ref):
        for t in range(hidden // LANES):
            part = first_ref[t * channels : (t + 1) * channels, :]
            w_in_ref[:, t * LANES : (t + 1) * LANES] = part.astype(F32) * factor
        for t in range(channels // LANES):
            part = second_ref[t * hidden : (t + 1) * hidden, :]
            w_out_ref[:, t * LANES : (t + 1) * LANES] = part.astype(F32) * factor

    @pl.when(core_ref[0] == 0)
    def _():
        write(mine_ref, other_ref)

    @pl.when(core_ref[0] != 0)
    def _():
        write(other_ref, mine_ref)


def shifts(axis, wrap):
    size = lax.axis_size(axis)
    up = [(i, (i + 1) % size) for i in range(size if wrap else size - 1)]
    return up, [(j, i) for i, j in up]


def halo_sides(field):
    rows, cols, _ = field.shape
    lat_up, lat_down = shifts(LAT, False)
    lon_up, lon_down = shifts(LON, True)
    up = lax.ppermute(field[rows - 3 :], LAT, lat_up)
    down = lax.ppermute(field[:3], LAT, lat_down)
    left = lax.ppermute(field[:, cols - 3 :], LON, lon_up)
    right = lax.ppermute(field[:, :3], LON, lon_down)
    return up, down, left, right


def halo_corners(left, right):
    rows = left.shape[0]
    lat_up, lat_down = shifts(LAT, False)
    sides = jnp.concatenate([left, right], axis=1)
    top = lax.ppermute(sides[rows - 3 :], LAT, lat_up)
    low = lax.ppermute(sides[:3], LAT, lat_down)
    return top, low


def local(
    ocean_state, land_sea, cotangent, dw_kernel, dw_bias, ln_gain, ln_bias, w_in, b_in, w_out, b_out, layer_scale
):
    _, rows, cols, channels = ocean_state.shape
    cells = rows * cols
    hidden = w_in.shape[1]
    far = lax.axis_size(FAR)
    core = lax.axis_index("core")
    own = ocean_state[0]
    cot = cotangent[0]
    up, down, left, right = halo_sides(own)
    top, low = halo_corners(left, right)
    mask = jnp.broadcast_to(land_sea[0].astype(BF16)[..., None], cot.shape)
    masked = mask * cot
    taps = dw_kernel.reshape(49, 2, LANES).transpose(1, 0, 2)
    pad = pltpu.VMEM((2, rows + 6, cols + 16, LANES), F32)
    plane = pltpu.VMEM((2, rows, cols, LANES), F32)
    params = pltpu.CompilerParams(vmem_limit_bytes=VMEM_BYTES)
    output, grad_depth, big, small = pl.pallas_call(
        block_kernel,
        out_shape=(
            jax.ShapeDtypeStruct((rows, cols, channels), BF16),
            jax.ShapeDtypeStruct((rows, cols, channels), BF16),
            jax.ShapeDtypeStruct((4 * hidden, LANES), BF16),
            jax.ShapeDtypeStruct((2, 64, LANES), F32),
        ),
        scratch_shapes=[pad, plane, pltpu.VMEM((2, 7, 7, 8, LANES), F32)],
        compiler_params=params,
        cost_estimate=pl.CostEstimate(flops=1300000000, transcendentals=400000, bytes_accessed=6000000),
        name="block",
    )(
        own, up, down, left, right, top, low, mask.reshape(cells, channels), masked.reshape(cells, channels), taps,
        dw_bias[None], ln_gain[None], ln_bias[None], w_in, b_in[None], w_out, b_out[None], layer_scale[None],
    )
    sides = halo_sides(grad_depth)
    small_rows = small.transpose(1, 0, 2).astype(BF16)
    small_rows = jnp.pad(small_rows, ((0, 2 * far - 64), (0, 0), (0, 0)))[:, None]
    chunks = jnp.concatenate([big.reshape(2 * far, 4, 2, LANES), small_rows], axis=1)
    pair = lax.all_to_all(chunks.reshape(2, far, 5, 2, LANES), "core", 0, 0)
    value = (pair[0].astype(F32) + pair[1].astype(F32)).astype(BF16)
    value = lax.all_to_all(value, FAR, 0, 0)
    value = jnp.sum(value.astype(F32), axis=0).astype(BF16)
    value, sides = lax.optimization_barrier((value, sides))
    value = lax.all_to_all(jnp.broadcast_to(value[None], (far, 5, 2, LANES)), FAR, 0, 0)
    g_up, g_down, g_left, g_right = sides
    g_top, g_low = halo_corners(g_left, g_right)
    grad_state = pl.pallas_call(
        state_kernel,
        out_shape=jax.ShapeDtypeStruct((rows, cols, channels), BF16),
        scratch_shapes=[pad, plane],
        compiler_params=params,
        cost_estimate=pl.CostEstimate(flops=10000000, transcendentals=0, bytes_accessed=3000000),
        name="state",
    )(grad_depth, g_up, g_down, g_left, g_right, g_top, g_low, cot, taps)
    value, grad_state = lax.optimization_barrier((value, grad_state))
    other = lax.ppermute(value, "core", [(0, 1), (1, 0)])
    total_cells = cells * lax.axis_size(LON) * lax.axis_size(LAT)
    factor = 1.0 / math.sqrt(total_cells)
    grad_w_in, grad_w_out = pl.pallas_call(
        functools.partial(unpack_kernel, factor),
        out_shape=(
            jax.ShapeDtypeStruct((channels, hidden), F32),
            jax.ShapeDtypeStruct((hidden, channels), F32),
        ),
        in_specs=[
            pl.BlockSpec(memory_space=pltpu.SMEM),
            pl.BlockSpec(memory_space=pltpu.VMEM),
            pl.BlockSpec(memory_space=pltpu.VMEM),
        ],
        compiler_params=params,
        name="unpack",
    )(
        core.astype(jnp.int32).reshape(1),
        value[:, :4].reshape(2 * hidden, LANES),
        other[:, :4].reshape(2 * hidden, LANES),
    )
    small_sum = jnp.where(core == 0, value[:64, 4], other[:64, 4]).astype(F32) * factor
    small_sum = small_sum.reshape(64, channels)
    blocks = hidden // channels
    singles = 49 + blocks
    grad_kernel = small_sum[:49].reshape(7, 7, channels).transpose(1, 0, 2)
    return (
        output[None],
        grad_state[None],
        grad_kernel,
        small_sum[singles],
        small_sum[singles + 1],
        small_sum[singles + 2],
        grad_w_in,
        small_sum[49:singles].reshape(hidden),
        grad_w_out,
        small_sum[singles + 3],
        small_sum[singles + 4],
    )


def solution(mesh):
    mesh = Mesh(mesh.devices.reshape(4, 2, 4, 2, 8), ("y_lo", "core", "x", "y_hi", "z"))
    field = P(None, LAT, LON, None)
    in_specs = (field, P(None, LAT, LON), field) + (P(),) * 9
    out_specs = (field, field) + (P(),) * 9
    return jax.shard_map(local, mesh=mesh, in_specs=in_specs, out_specs=out_specs, check_vma=False)
```

```python
import functools
import math

import jax
import jax.numpy as jnp
from jax import lax
from jax.experimental import pallas as pl
from jax.experimental.pallas import tpu as pltpu
from jax.sharding import Mesh, PartitionSpec as P

LON = ("y_lo", "core")
LAT = ("x", "y_hi", "z")
FAR = ("x", "y_hi", "y_lo", "z")
LANES = 128
VMEM_BYTES = 44 << 20
F32 = jnp.float32
BF16 = jnp.bfloat16


def dot(a, b, ca, cb):
    return lax.dot_general(a, b, (((ca,), (cb,)), ((), ())), preferred_element_type=F32)


def fill_padded(odd_ref, pad_ref, own_ref, near_rows_ref, far_rows_ref, near_cols_ref, far_cols_ref):
    rows, cols, _ = own_ref.shape
    low = rows + 3
    near_at = jnp.where(odd_ref[0] == 1, 0, low)
    far_at = low - near_at
    for t in range(2):
        ln = slice(t * LANES, (t + 1) * LANES)
        pad_ref[t, 3 : 3 + rows, 8 : 8 + cols] = own_ref[:, :, ln].astype(F32)
        pad_ref[t, pl.ds(near_at, 3), 8 : 8 + cols] = near_rows_ref[:, :, ln].astype(F32)
        pad_ref[t, pl.ds(far_at, 3), 8 : 8 + cols] = far_rows_ref[:, :, ln].astype(F32)

    def place(left_ref, right_ref):
        for t in range(2):
            ln = slice(t * LANES, (t + 1) * LANES)
            pad_ref[t, :, 5:8] = left_ref[:, :, ln].astype(F32)
            pad_ref[t, :, 8 + cols : 11 + cols] = right_ref[:, :, ln].astype(F32)

    @pl.when(odd_ref[1] == 0)
    def _():
        place(far_cols_ref, near_cols_ref)

    @pl.when(odd_ref[1] != 0)
    def _():
        place(near_cols_ref, far_cols_ref)


def convolve(pad_ref, k_ref, out_ref, rows, cols, flip):
    blocks = cols // 8

    def step(n, carry):
        t = n // blocks
        at = pl.multiple_of((n % blocks) * 8, 8)
        acc = [jnp.zeros((8, LANES), F32) for _ in range(rows)]
        for j in range(7):
            window = [pad_ref[t, r, pl.ds(at + 5 + j, 8), :] for r in range(rows + 6)]
            for i in range(7):
                tap = (6 - i) * 7 + 6 - j if flip else i * 7 + j
                weight = k_ref[t, tap : tap + 1, :]
                for p in range(rows):
                    acc[p] = acc[p] + window[p + i] * weight
        for p in range(rows):
            out_ref[t, p, pl.ds(at, 8), :] = acc[p]
        return carry

    lax.fori_loop(0, 2 * blocks, step, 0)


def kernel_sums(pad_ref, grad_ref, out_ref, rows, cols):
    def step(n, carry):
        t, j = n // 7, n % 7
        acc = [jnp.zeros((8, LANES), F32) for _ in range(7)]
        for b in range(cols // 8):
            window = [pad_ref[t, r, pl.ds(b * 8 + 5 + j, 8), :] for r in range(rows + 6)]
            grad = [grad_ref[t, p, b * 8 : b * 8 + 8, :] for p in range(rows)]
            for i in range(7):
                for p in range(rows):
                    acc[i] = acc[i] + window[p + i] * grad[p]
        for i in range(7):
            out_ref[t, j, i] = acc[i]
        return carry

    lax.fori_loop(0, 14, step, 0)


def block_kernel(
    odd_ref, own_ref, near_rows_ref, far_rows_ref, near_cols_ref, far_cols_ref, mask_ref, masked_ref, k_ref, dw_bias_ref,
    gain_ref, bias_ref, w_in_ref, b_in_ref, w_out_ref, b_out_ref, scale_ref,
    out_ref, grad_ref, big_ref, small_ref,
    pad_ref, depth_ref, terms_ref,
):
    rows, cols, channels = own_ref.shape
    cells = rows * cols
    hidden = w_in_ref.shape[1]
    halves = channels // LANES
    fill_padded(odd_ref, pad_ref, own_ref, near_rows_ref, far_rows_ref, near_cols_ref, far_cols_ref)
    convolve(pad_ref, k_ref, depth_ref, rows, cols, False)
    depth = jnp.concatenate([depth_ref[t].reshape(cells, LANES) for t in range(2)], axis=1)
    depth = depth + dw_bias_ref[...]
    center = depth - jnp.mean(depth, axis=-1, keepdims=True)
    inv_std = lax.rsqrt(jnp.mean(center * center, axis=-1, keepdims=True) + 1e-6)
    norm_hat = center * inv_std
    normed = (norm_hat * gain_ref[...] + bias_ref[...]).astype(BF16)
    masked = masked_ref[...].astype(F32)
    grad_branch = (masked * scale_ref[...]).astype(BF16)
    branch = jnp.zeros((cells, channels), F32)
    grad_norm = jnp.zeros((cells, channels), F32)
    root = math.sqrt(2.0 / math.pi)
    b_in_sums = []
    width = channels
    for h in range(hidden // width):
        at = slice(h * width, (h + 1) * width)
        w_in = w_in_ref[:, at]
        w_out = w_out_ref[at, :]
        pre = dot(normed, w_in, 1, 0) + b_in_ref[:, at]
        square = pre * pre
        bent = jnp.tanh(root * pre * (1.0 + 0.044715 * square))
        half = 0.5 * (1.0 + bent)
        act = (pre * half).astype(BF16)
        slope = half + (0.5 * root) * pre * (1.0 - bent * bent) * (1.0 + (3 * 0.044715) * square)
        grad_pre = (dot(grad_branch, w_out, 1, 1) * slope).astype(BF16)
        branch = branch + dot(act, w_out, 1, 0)
        grad_norm = grad_norm + dot(grad_pre, w_in, 1, 1)
        g_in = dot(normed, grad_pre, 0, 0).astype(BF16)
        g_out = dot(act, grad_branch, 0, 0).astype(BF16)
        for t in range(width // LANES):
            base = (h * (width // LANES) + t) * channels
            big_ref[base : base + channels, :] = g_in[:, t * LANES : (t + 1) * LANES]
        for t in range(halves):
            base = hidden * halves + t * hidden + h * width
            big_ref[base : base + width, :] = g_out[:, t * LANES : (t + 1) * LANES]
        b_in_sums.append(jnp.sum(grad_pre.astype(F32), axis=0, keepdims=True))
    branch = branch + b_out_ref[...]
    mask = mask_ref[...].astype(F32)
    own = own_ref[...].reshape(cells, channels).astype(F32)
    out_ref[...] = (own + mask * scale_ref[...] * branch).astype(BF16).reshape(rows, cols, channels)
    scaled = grad_norm * gain_ref[...]
    mean_u = jnp.mean(scaled, axis=-1, keepdims=True)
    mean_un = jnp.mean(scaled * norm_hat, axis=-1, keepdims=True)
    grad_depth = (inv_std * (scaled - mean_u - norm_hat * mean_un)).astype(BF16)
    grad_ref[...] = grad_depth.reshape(rows, cols, channels)
    grad_float = grad_depth.astype(F32)
    for t in range(2):
        depth_ref[t] = grad_float[:, t * LANES : (t + 1) * LANES].reshape(rows, cols, LANES)
    kernel_sums(pad_ref, depth_ref, terms_ref, rows, cols)
    singles = b_in_sums + [
        jnp.sum(grad_float, axis=0, keepdims=True),
        jnp.sum(grad_norm * norm_hat, axis=0, keepdims=True),
        jnp.sum(grad_norm, axis=0, keepdims=True),
        jnp.sum(grad_branch.astype(F32), axis=0, keepdims=True),
        jnp.sum(masked * branch, axis=0, keepdims=True),
    ]
    for t in range(2):
        ln = slice(t * LANES, (t + 1) * LANES)
        small_ref[t, 0:49, :] = jnp.sum(terms_ref[t].reshape(49, 8, LANES), axis=1)
        for n, single in enumerate(singles):
            small_ref[t, 49 + n : 50 + n, :] = single[:, ln]
        small_ref[t, 49 + len(singles) :, :] = jnp.zeros((64 - 49 - len(singles), LANES), F32)


def state_kernel(
    odd_ref, own_ref, near_rows_ref, far_rows_ref, near_cols_ref, far_cols_ref, cot_ref, k_ref, out_ref, pad_ref, sum_ref
):
    rows, cols, _ = own_ref.shape
    fill_padded(odd_ref, pad_ref, own_ref, near_rows_ref, far_rows_ref, near_cols_ref, far_cols_ref)
    convolve(pad_ref, k_ref, sum_ref, rows, cols, True)
    for t in range(2):
        ln = slice(t * LANES, (t + 1) * LANES)
        out_ref[:, :, ln] = (cot_ref[:, :, ln].astype(F32) + sum_ref[t]).astype(BF16)


def unpack_kernel(factor, core_ref, mine_ref, other_ref, w_in_ref, w_out_ref):
    channels, hidden = w_in_ref.shape

    def write(first_ref, second_ref):
        for t in range(hidden // LANES):
            part = first_ref[t * channels : (t + 1) * channels, :]
            w_in_ref[:, t * LANES : (t + 1) * LANES] = part.astype(F32) * factor
        for t in range(channels // LANES):
            part = second_ref[t * hidden : (t + 1) * hidden, :]
            w_out_ref[:, t * LANES : (t + 1) * LANES] = part.astype(F32) * factor

    @pl.when(core_ref[0] == 0)
    def _():
        write(mine_ref, other_ref)

    @pl.when(core_ref[0] != 0)
    def _():
        write(other_ref, mine_ref)


def swaps(axis, wrap):
    size = lax.axis_size(axis)
    near = [(i, i ^ 1) for i in range(size)]
    far = []
    for i in range(1, size if wrap else size - 1, 2):
        far += [(i, (i + 1) % size), ((i + 1) % size, i)]
    return near, far


def swap_rows(field, odd):
    rows = field.shape[0]
    near, far = swaps(LAT, False)
    first, last = field[:3], field[rows - 3 :]
    far_rows = lax.ppermute(jnp.where(odd, last, first), LAT, far)
    near_rows = lax.ppermute(jnp.where(odd, first, last), LAT, near)
    return near_rows, far_rows


def swap_cols(field, near_rows, far_rows, odd_lat, odd_lon):
    cols = field.shape[1]
    near, far = swaps(LON, True)

    def strip(at):
        part = slice(at, at + 3)
        before = jnp.where(odd_lat, near_rows[:, part], far_rows[:, part])
        after = jnp.where(odd_lat, far_rows[:, part], near_rows[:, part])
        return jnp.concatenate([before, field[:, part], after], axis=0)

    first, last = strip(0), strip(cols - 3)
    far_cols = lax.ppermute(jnp.where(odd_lon, last, first), LON, far)
    near_cols = lax.ppermute(jnp.where(odd_lon, first, last), LON, near)
    return near_cols, far_cols


def local(
    ocean_state, land_sea, cotangent, dw_kernel, dw_bias, ln_gain, ln_bias, w_in, b_in, w_out, b_out, layer_scale
):
    _, rows, cols, channels = ocean_state.shape
    cells = rows * cols
    hidden = w_in.shape[1]
    far = lax.axis_size(FAR)
    core = lax.axis_index("core")
    own = ocean_state[0]
    cot = cotangent[0]
    odd_lat = lax.axis_index("z") & 1
    odd = jnp.stack([odd_lat, core]).astype(jnp.int32)
    odd_lat, odd_lon = odd_lat == 1, core == 1
    near_rows, far_rows = swap_rows(own, odd_lat)
    near_cols, far_cols = swap_cols(own, near_rows, far_rows, odd_lat, odd_lon)
    mask = jnp.broadcast_to(land_sea[0].astype(BF16)[..., None], cot.shape)
    masked = mask * cot
    taps = dw_kernel.reshape(49, 2, LANES).transpose(1, 0, 2)
    pad = pltpu.VMEM((2, rows + 6, cols + 16, LANES), F32)
    plane = pltpu.VMEM((2, rows, cols, LANES), F32)
    smem, vmem = pl.BlockSpec(memory_space=pltpu.SMEM), pl.BlockSpec(memory_space=pltpu.VMEM)
    params = pltpu.CompilerParams(vmem_limit_bytes=VMEM_BYTES)
    output, grad_depth, big, small = pl.pallas_call(
        block_kernel,
        out_shape=(
            jax.ShapeDtypeStruct((rows, cols, channels), BF16),
            jax.ShapeDtypeStruct((rows, cols, channels), BF16),
            jax.ShapeDtypeStruct((4 * hidden, LANES), BF16),
            jax.ShapeDtypeStruct((2, 64, LANES), F32),
        ),
        in_specs=[smem] + [vmem] * 16,
        scratch_shapes=[pad, plane, pltpu.VMEM((2, 7, 7, 8, LANES), F32)],
        compiler_params=params,
        cost_estimate=pl.CostEstimate(flops=1300000000, transcendentals=400000, bytes_accessed=6000000),
        name="block",
    )(
        odd, own, near_rows, far_rows, near_cols, far_cols, mask.reshape(cells, channels), masked.reshape(cells, channels), taps,
        dw_bias[None], ln_gain[None], ln_bias[None], w_in, b_in[None], w_out, b_out[None], layer_scale[None],
    )
    rows_sent = swap_rows(grad_depth, odd_lat)
    small_rows = small.transpose(1, 0, 2).astype(BF16)
    small_rows = jnp.pad(small_rows, ((0, 2 * far - 64), (0, 0), (0, 0)))[:, None]
    chunks = jnp.concatenate([big.reshape(2 * far, 4, 2, LANES), small_rows], axis=1)
    pair = lax.all_to_all(chunks.reshape(2, far * 10, LANES), "core", 0, 0)
    value = (pair[0].astype(F32) + pair[1].astype(F32)).astype(BF16)
    value = lax.all_to_all(value.reshape(far, 5, 2, LANES), FAR, 0, 0)
    value = jnp.sum(value.astype(F32), axis=0).astype(BF16)
    value, rows_sent = lax.optimization_barrier((value, rows_sent))
    value = lax.all_to_all(jnp.broadcast_to(value[None], (far, 5, 2, LANES)), FAR, 0, 0)
    cols_sent = swap_cols(grad_depth, *rows_sent, odd_lat, odd_lon)
    grad_state = pl.pallas_call(
        state_kernel,
        out_shape=jax.ShapeDtypeStruct((rows, cols, channels), BF16),
        in_specs=[smem] + [vmem] * 7,
        scratch_shapes=[pad, plane],
        compiler_params=params,
        cost_estimate=pl.CostEstimate(flops=10000000, transcendentals=0, bytes_accessed=3000000),
        name="state",
    )(odd, grad_depth, *rows_sent, *cols_sent, cot, taps)
    value, grad_state = lax.optimization_barrier((value, grad_state))
    other = lax.ppermute(value, "core", [(0, 1), (1, 0)])
    total_cells = cells * lax.axis_size(LON) * lax.axis_size(LAT)
    factor = 1.0 / math.sqrt(total_cells)
    grad_w_in, grad_w_out = pl.pallas_call(
        functools.partial(unpack_kernel, factor),
        out_shape=(
            jax.ShapeDtypeStruct((channels, hidden), F32),
            jax.ShapeDtypeStruct((hidden, channels), F32),
        ),
        in_specs=[smem, vmem, vmem],
        compiler_params=params,
        name="unpack",
    )(
        core.astype(jnp.int32).reshape(1),
        value[:, :4].reshape(2 * hidden, LANES),
        other[:, :4].reshape(2 * hidden, LANES),
    )
    small_sum = jnp.where(core == 0, value[:64, 4], other[:64, 4]).astype(F32) * factor
    small_sum = small_sum.reshape(64, channels)
    blocks = hidden // channels
    singles = 49 + blocks
    grad_kernel = small_sum[:49].reshape(7, 7, channels).transpose(1, 0, 2)
    return (
        output[None],
        grad_state[None],
        grad_kernel,
        small_sum[singles],
        small_sum[singles + 1],
        small_sum[singles + 2],
        grad_w_in,
        small_sum[49:singles].reshape(hidden),
        grad_w_out,
        small_sum[singles + 3],
        small_sum[singles + 4],
    )


def solution(mesh):
    mesh = Mesh(mesh.devices.reshape(4, 2, 4, 2, 8), ("y_lo", "core", "x", "y_hi", "z"))
    field = P(None, LAT, LON, None)
    in_specs = (field, P(None, LAT, LON), field) + (P(),) * 9
    out_specs = (field, field) + (P(),) * 9
    return jax.shard_map(local, mesh=mesh, in_specs=in_specs, out_specs=out_specs, check_vma=False)
```

```python
import functools
import math

import jax
import jax.numpy as jnp
from jax import lax
from jax.experimental import pallas as pl
from jax.experimental.pallas import tpu as pltpu
from jax.sharding import Mesh, PartitionSpec as P

LON = ("y_lo", "core")
LAT = ("x", "y_hi", "z")
PLANE = ("x", "z")
COLUMN = ("y_hi", "y_lo")
BIG_ROWS = 64
CHUNK_ROWS = 72
LANES = 128
VMEM_BYTES = 44 << 20
F32 = jnp.float32
BF16 = jnp.bfloat16


def dot(a, b, ca, cb):
    return lax.dot_general(a, b, (((ca,), (cb,)), ((), ())), preferred_element_type=F32)


def fill_padded(odd_ref, pad_ref, own_ref, near_rows_ref, far_rows_ref, near_cols_ref, far_cols_ref):
    rows, cols, _ = own_ref.shape
    low = rows + 3
    near_at = jnp.where(odd_ref[0] == 1, 0, low)
    far_at = low - near_at
    for t in range(2):
        ln = slice(t * LANES, (t + 1) * LANES)
        pad_ref[t, 3 : 3 + rows, 8 : 8 + cols] = own_ref[:, :, ln].astype(F32)
        pad_ref[t, pl.ds(near_at, 3), 8 : 8 + cols] = near_rows_ref[:, :, ln].astype(F32)
        pad_ref[t, pl.ds(far_at, 3), 8 : 8 + cols] = far_rows_ref[:, :, ln].astype(F32)

    def place(left_ref, right_ref):
        for t in range(2):
            ln = slice(t * LANES, (t + 1) * LANES)
            pad_ref[t, :, 5:8] = left_ref[:, :, ln].astype(F32)
            pad_ref[t, :, 8 + cols : 11 + cols] = right_ref[:, :, ln].astype(F32)

    @pl.when(odd_ref[1] == 0)
    def _():
        place(far_cols_ref, near_cols_ref)

    @pl.when(odd_ref[1] != 0)
    def _():
        place(near_cols_ref, far_cols_ref)


def convolve(pad_ref, k_ref, out_ref, rows, cols, flip):
    for t in range(2):
        ln = slice(t * LANES, (t + 1) * LANES)

        def step(n, carry, t=t, ln=ln):
            at = pl.multiple_of(n * 8, 8)
            acc = [jnp.zeros((8, LANES), F32) for _ in range(rows)]
            for j in range(7):
                window = [pad_ref[t, r, pl.ds(at + 5 + j, 8), :] for r in range(rows + 6)]
                for i in range(7):
                    row, col = (6 - i, 6 - j) if flip else (i, j)
                    weight = k_ref[row, col : col + 1, ln]
                    for p in range(rows):
                        acc[p] = acc[p] + window[p + i] * weight
            for p in range(rows):
                out_ref[t, p, pl.ds(at, 8), :] = acc[p]
            return carry

        lax.fori_loop(0, cols // 8, step, 0)


def kernel_sums(pad_ref, grad_ref, out_ref, rows, cols):
    def step(n, carry):
        t, j = n // 7, n % 7
        acc = [jnp.zeros((8, LANES), F32) for _ in range(7)]
        for b in range(cols // 8):
            window = [pad_ref[t, r, pl.ds(b * 8 + 5 + j, 8), :] for r in range(rows + 6)]
            grad = [grad_ref[t, p, b * 8 : b * 8 + 8, :] for p in range(rows)]
            for i in range(7):
                for p in range(rows):
                    acc[i] = acc[i] + window[p + i] * grad[p]
        for i in range(7):
            out_ref[t, j, i] = acc[i]
        return carry

    lax.fori_loop(0, 14, step, 0)


def write_chunks(chunk_ref, base, part):
    for n in range(part.shape[0] // BIG_ROWS):
        chunk_ref[base + n, 0:BIG_ROWS, :] = part[n * BIG_ROWS : (n + 1) * BIG_ROWS]


def block_kernel(
    odd_ref, own_ref, near_rows_ref, far_rows_ref, near_cols_ref, far_cols_ref, mask_ref, masked_ref, k_ref, dw_bias_ref,
    gain_ref, bias_ref, w_in_ref, b_in_ref, w_out_ref, b_out_ref, scale_ref,
    out_ref, grad_ref, chunk_ref,
    pad_ref, depth_ref, terms_ref, small_ref,
):
    rows, cols, channels = own_ref.shape
    cells = rows * cols
    hidden = w_in_ref.shape[1]
    halves = channels // LANES
    fill_padded(odd_ref, pad_ref, own_ref, near_rows_ref, far_rows_ref, near_cols_ref, far_cols_ref)
    convolve(pad_ref, k_ref, depth_ref, rows, cols, False)
    depth = jnp.concatenate([depth_ref[t].reshape(cells, LANES) for t in range(2)], axis=1)
    depth = depth + dw_bias_ref[...]
    center = depth - jnp.mean(depth, axis=-1, keepdims=True)
    inv_std = lax.rsqrt(jnp.mean(center * center, axis=-1, keepdims=True) + 1e-6)
    norm_hat = center * inv_std
    normed = (norm_hat * gain_ref[...] + bias_ref[...]).astype(BF16)
    masked = masked_ref[...].astype(F32)
    grad_branch = (masked * scale_ref[...]).astype(BF16)
    branch = jnp.zeros((cells, channels), F32)
    grad_norm = jnp.zeros((cells, channels), F32)
    root = math.sqrt(2.0 / math.pi)
    b_in_sums = []
    width = channels
    for h in range(hidden // width):
        at = slice(h * width, (h + 1) * width)
        w_in = w_in_ref[:, at]
        w_out = w_out_ref[at, :]
        pre = dot(normed, w_in, 1, 0) + b_in_ref[:, at]
        square = pre * pre
        bent = jnp.tanh(root * pre * (1.0 + 0.044715 * square))
        half = 0.5 * (1.0 + bent)
        act = (pre * half).astype(BF16)
        slope = half + (0.5 * root) * pre * (1.0 - bent * bent) * (1.0 + (3 * 0.044715) * square)
        grad_pre = (dot(grad_branch, w_out, 1, 1) * slope).astype(BF16)
        branch = branch + dot(act, w_out, 1, 0)
        grad_norm = grad_norm + dot(grad_pre, w_in, 1, 1)
        g_in = dot(normed, grad_pre, 0, 0).astype(BF16)
        g_out = dot(act, grad_branch, 0, 0).astype(BF16)
        for t in range(width // LANES):
            base = (h * (width // LANES) + t) * (channels // BIG_ROWS)
            write_chunks(chunk_ref, base, g_in[:, t * LANES : (t + 1) * LANES])
        for t in range(halves):
            base = (hidden * halves + t * hidden + h * width) // BIG_ROWS
            write_chunks(chunk_ref, base, g_out[:, t * LANES : (t + 1) * LANES])
        b_in_sums.append(jnp.sum(grad_pre.astype(F32), axis=0, keepdims=True))
    branch = branch + b_out_ref[...]
    mask = mask_ref[...].astype(F32)
    own = own_ref[...].reshape(cells, channels).astype(F32)
    out_ref[...] = (own + mask * scale_ref[...] * branch).astype(BF16).reshape(rows, cols, channels)
    scaled = grad_norm * gain_ref[...]
    mean_u = jnp.mean(scaled, axis=-1, keepdims=True)
    mean_un = jnp.mean(scaled * norm_hat, axis=-1, keepdims=True)
    grad_depth = (inv_std * (scaled - mean_u - norm_hat * mean_un)).astype(BF16)
    grad_ref[...] = grad_depth.reshape(rows, cols, channels)
    grad_float = grad_depth.astype(F32)
    for t in range(2):
        depth_ref[t] = grad_float[:, t * LANES : (t + 1) * LANES].reshape(rows, cols, LANES)
    kernel_sums(pad_ref, depth_ref, terms_ref, rows, cols)
    singles = b_in_sums + [
        jnp.sum(grad_float, axis=0, keepdims=True),
        jnp.sum(grad_norm * norm_hat, axis=0, keepdims=True),
        jnp.sum(grad_norm, axis=0, keepdims=True),
        jnp.sum(grad_branch.astype(F32), axis=0, keepdims=True),
        jnp.sum(masked * branch, axis=0, keepdims=True),
    ]
    for t in range(2):
        ln = slice(t * LANES, (t + 1) * LANES)
        small_ref[t, 0:49, :] = jnp.sum(terms_ref[t].reshape(49, 8, LANES), axis=1)
        for n, single in enumerate(singles):
            small_ref[t, 49 + n : 50 + n, :] = single[:, ln]
        small_ref[t, 49 + len(singles) :, :] = jnp.zeros((64 - 49 - len(singles), LANES), F32)
    chunks = chunk_ref.shape[0]
    for c in range(chunks):
        n = c % (chunks // 2)
        if n < 16:
            piece = small_ref[n // 8, (n % 8) * 8 : (n % 8) * 8 + 8, :].astype(BF16)
        else:
            piece = jnp.zeros((8, LANES), BF16)
        chunk_ref[c, BIG_ROWS:, :] = piece


def state_kernel(
    odd_ref, own_ref, near_rows_ref, far_rows_ref, near_cols_ref, far_cols_ref, cot_ref, k_ref, out_ref, pad_ref, sum_ref
):
    rows, cols, _ = own_ref.shape
    fill_padded(odd_ref, pad_ref, own_ref, near_rows_ref, far_rows_ref, near_cols_ref, far_cols_ref)
    convolve(pad_ref, k_ref, sum_ref, rows, cols, True)
    for t in range(2):
        ln = slice(t * LANES, (t + 1) * LANES)
        out_ref[:, :, ln] = (cot_ref[:, :, ln].astype(F32) + sum_ref[t]).astype(BF16)


def unpack_kernel(
    factor, core_ref, mine_ref, other_ref, k_ref, singles_ref, w_in_ref, b_in_ref, w_out_ref, small_ref
):
    channels, hidden = w_in_ref.shape

    def rows_of(ref, at, size):
        part = ref[at // BIG_ROWS : (at + size) // BIG_ROWS, 0:BIG_ROWS, :]
        return part.astype(F32).reshape(size, LANES) * factor

    def write(first_ref, second_ref):
        for t in range(hidden // LANES):
            w_in_ref[:, t * LANES : (t + 1) * LANES] = rows_of(first_ref, t * channels, channels)
        for t in range(channels // LANES):
            w_out_ref[:, t * LANES : (t + 1) * LANES] = rows_of(second_ref, t * hidden, hidden)

    @pl.when(core_ref[0] == 0)
    def _():
        write(mine_ref, other_ref)

    @pl.when(core_ref[0] != 0)
    def _():
        write(other_ref, mine_ref)

    small_ref[...] = mine_ref[0:16, BIG_ROWS:, :].astype(F32).reshape(128, LANES) * factor
    blocks = hidden // channels
    for t in range(2):
        ln = slice(t * LANES, (t + 1) * LANES)
        for j in range(7):
            for i in range(7):
                at = t * 64 + j * 7 + i
                k_ref[i, j : j + 1, ln] = small_ref[at : at + 1, :]
        at = t * 64 + 49
        for n in range(blocks):
            part = slice(n * channels + t * LANES, n * channels + (t + 1) * LANES)
            b_in_ref[:, part] = small_ref[at + n : at + n + 1, :]
        for n in range(5):
            singles_ref[n, :, ln] = small_ref[at + blocks + n : at + blocks + n + 1, :]


def swaps(axis, wrap):
    size = lax.axis_size(axis)
    near = [(i, i ^ 1) for i in range(size)]
    far = []
    for i in range(1, size if wrap else size - 1, 2):
        far += [(i, (i + 1) % size), ((i + 1) % size, i)]
    return near, far


def swap_rows(field, odd):
    rows = field.shape[0]
    near, far = swaps(LAT, False)
    first, last = field[:3], field[rows - 3 :]
    far_rows = lax.ppermute(jnp.where(odd, last, first), LAT, far)
    near_rows = lax.ppermute(jnp.where(odd, first, last), LAT, near)
    return near_rows, far_rows


def swap_cols(field, near_rows, far_rows, odd_lat, odd_lon):
    cols = field.shape[1]
    near, far = swaps(LON, True)

    def strip(at):
        part = slice(at, at + 3)
        before = jnp.where(odd_lat, near_rows[:, part], far_rows[:, part])
        after = jnp.where(odd_lat, far_rows[:, part], near_rows[:, part])
        return jnp.concatenate([before, field[:, part], after], axis=0)

    first, last = strip(0), strip(cols - 3)
    far_cols = lax.ppermute(jnp.where(odd_lon, last, first), LON, far)
    near_cols = lax.ppermute(jnp.where(odd_lon, first, last), LON, near)
    return near_cols, far_cols


def local(
    ocean_state, land_sea, cotangent, dw_kernel, dw_bias, ln_gain, ln_bias, w_in, b_in, w_out, b_out, layer_scale
):
    _, rows, cols, channels = ocean_state.shape
    cells = rows * cols
    hidden = w_in.shape[1]
    plane, column = lax.axis_size(PLANE), lax.axis_size(COLUMN)
    core = lax.axis_index("core")
    own = ocean_state[0]
    cot = cotangent[0]
    odd_lat = lax.axis_index("z") & 1
    odd = jnp.stack([odd_lat, core]).astype(jnp.int32)
    odd_lat, odd_lon = odd_lat == 1, core == 1
    near_rows, far_rows = swap_rows(own, odd_lat)
    near_cols, far_cols = swap_cols(own, near_rows, far_rows, odd_lat, odd_lon)
    mask = jnp.broadcast_to(land_sea[0].astype(BF16)[..., None], cot.shape)
    masked = mask * cot
    pad = pltpu.VMEM((2, rows + 6, cols + 16, LANES), F32)
    cells_scratch = pltpu.VMEM((2, rows, cols, LANES), F32)
    smem, vmem = pl.BlockSpec(memory_space=pltpu.SMEM), pl.BlockSpec(memory_space=pltpu.VMEM)
    params = pltpu.CompilerParams(vmem_limit_bytes=VMEM_BYTES)
    output, grad_depth, chunks = pl.pallas_call(
        block_kernel,
        out_shape=(
            jax.ShapeDtypeStruct((rows, cols, channels), BF16),
            jax.ShapeDtypeStruct((rows, cols, channels), BF16),
            jax.ShapeDtypeStruct((2 * plane, CHUNK_ROWS, LANES), BF16),
        ),
        in_specs=[smem] + [vmem] * 16,
        scratch_shapes=[
            pad,
            cells_scratch,
            pltpu.VMEM((2, 7, 7, 8, LANES), F32),
            pltpu.VMEM((2, 64, LANES), F32),
        ],
        compiler_params=params,
        cost_estimate=pl.CostEstimate(flops=1300000000, transcendentals=400000, bytes_accessed=6000000),
        name="block",
    )(
        odd, own, near_rows, far_rows, near_cols, far_cols, mask.reshape(cells, channels), masked.reshape(cells, channels), dw_kernel,
        dw_bias[None], ln_gain[None], ln_bias[None], w_in, b_in[None], w_out, b_out[None], layer_scale[None],
    )
    rows_sent = swap_rows(grad_depth, odd_lat)
    pair = lax.all_to_all(chunks.reshape(2, plane, CHUNK_ROWS, LANES), "core", 0, 0)
    value = (pair[0].astype(F32) + pair[1].astype(F32)).astype(BF16)
    value = lax.all_to_all(value, PLANE, 0, 0)
    value = jnp.sum(value.astype(F32), axis=0).astype(BF16)
    value, rows_sent = lax.optimization_barrier((value, rows_sent))
    value = lax.all_to_all(jnp.broadcast_to(value[None], (column,) + value.shape), COLUMN, 0, 0)
    value = jnp.sum(value.astype(F32), axis=0).astype(BF16)
    value = lax.all_to_all(jnp.broadcast_to(value[None], (plane,) + value.shape), PLANE, 0, 0)
    cols_sent = swap_cols(grad_depth, *rows_sent, odd_lat, odd_lon)
    grad_state = pl.pallas_call(
        state_kernel,
        out_shape=jax.ShapeDtypeStruct((rows, cols, channels), BF16),
        in_specs=[smem] + [vmem] * 7,
        scratch_shapes=[pad, cells_scratch],
        compiler_params=params,
        cost_estimate=pl.CostEstimate(flops=10000000, transcendentals=0, bytes_accessed=3000000),
        name="state",
    )(odd, grad_depth, *rows_sent, *cols_sent, cot, dw_kernel)
    value, grad_state = lax.optimization_barrier((value, grad_state))
    other = lax.ppermute(value, "core", [(0, 1), (1, 0)])
    total_cells = cells * lax.axis_size(LON) * lax.axis_size(LAT)
    factor = 1.0 / math.sqrt(total_cells)
    grad_kernel, singles, grad_w_in, grad_b_in, grad_w_out = pl.pallas_call(
        functools.partial(unpack_kernel, factor),
        out_shape=(
            jax.ShapeDtypeStruct(dw_kernel.shape, F32),
            jax.ShapeDtypeStruct((5, 1, channels), F32),
            jax.ShapeDtypeStruct((channels, hidden), F32),
            jax.ShapeDtypeStruct((1, hidden), F32),
            jax.ShapeDtypeStruct((hidden, channels), F32),
        ),
        in_specs=[smem, vmem, vmem],
        scratch_shapes=[pltpu.VMEM((128, LANES), F32)],
        compiler_params=params,
        name="unpack",
    )(core.astype(jnp.int32).reshape(1), value, other)
    return (
        output[None],
        grad_state[None],
        grad_kernel,
        singles[0, 0],
        singles[1, 0],
        singles[2, 0],
        grad_w_in,
        grad_b_in[0],
        grad_w_out,
        singles[3, 0],
        singles[4, 0],
    )


def solution(mesh):
    mesh = Mesh(mesh.devices.reshape(4, 2, 4, 2, 8), ("y_lo", "core", "x", "y_hi", "z"))
    field = P(None, LAT, LON, None)
    in_specs = (field, P(None, LAT, LON), field) + (P(),) * 9
    out_specs = (field, field) + (P(),) * 9
    return jax.shard_map(local, mesh=mesh, in_specs=in_specs, out_specs=out_specs, check_vma=False)
```

```python
import functools
import math

import jax
import jax.numpy as jnp
import numpy as np
from jax import lax
from jax.experimental import pallas as pl
from jax.experimental.pallas import tpu as pltpu
from jax.sharding import Mesh, PartitionSpec as P

LON = ("y_lo", "core")
LAT = ("x", "y_hi", "z")
SIZES = {"y_lo": 4, "core": 2, "x": 4, "y_hi": 2, "z": 8}
EVERY = tuple(SIZES)
BIG_ROWS = 64
CHUNK_ROWS = 72
LANES = 128
VMEM_BYTES = 32 << 20
F32 = jnp.float32
BF16 = jnp.bfloat16


def dot(a, b, ca, cb):
    return lax.dot_general(a, b, (((ca,), (cb,)), ((), ())), preferred_element_type=F32)


def fill_padded(odd_ref, pad_ref, own_ref, near_rows_ref, far_rows_ref, near_cols_ref, far_cols_ref):
    rows, cols, _ = own_ref.shape
    low = rows + 3
    near_at = jnp.where(odd_ref[0] == 1, 0, low)
    far_at = low - near_at
    for t in range(2):
        ln = slice(t * LANES, (t + 1) * LANES)
        pad_ref[t, 3 : 3 + rows, 8 : 8 + cols] = own_ref[:, :, ln].astype(F32)
        pad_ref[t, pl.ds(near_at, 3), 8 : 8 + cols] = near_rows_ref[:, :, ln].astype(F32)
        pad_ref[t, pl.ds(far_at, 3), 8 : 8 + cols] = far_rows_ref[:, :, ln].astype(F32)

    def place(left_ref, right_ref):
        for t in range(2):
            ln = slice(t * LANES, (t + 1) * LANES)
            pad_ref[t, :, 5:8] = left_ref[:, :, ln].astype(F32)
            pad_ref[t, :, 8 + cols : 11 + cols] = right_ref[:, :, ln].astype(F32)

    @pl.when(odd_ref[1] == 0)
    def _():
        place(far_cols_ref, near_cols_ref)

    @pl.when(odd_ref[1] != 0)
    def _():
        place(near_cols_ref, far_cols_ref)


def convolve(pad_ref, k_ref, out_ref, rows, cols, flip):
    for t in range(2):
        ln = slice(t * LANES, (t + 1) * LANES)

        def step(n, carry, t=t, ln=ln):
            at = pl.multiple_of(n * 8, 8)
            acc = [jnp.zeros((8, LANES), F32) for _ in range(rows)]
            for j in range(7):
                window = [pad_ref[t, r, pl.ds(at + 5 + j, 8), :] for r in range(rows + 6)]
                for i in range(7):
                    row, col = (6 - i, 6 - j) if flip else (i, j)
                    weight = k_ref[row, col : col + 1, ln]
                    for p in range(rows):
                        acc[p] = acc[p] + window[p + i] * weight
            for p in range(rows):
                out_ref[t, p, pl.ds(at, 8), :] = acc[p]
            return carry

        lax.fori_loop(0, cols // 8, step, 0)


def kernel_sums(pad_ref, grad_ref, out_ref, rows, cols):
    def step(n, carry):
        t, j = n // 7, n % 7
        acc = [jnp.zeros((8, LANES), F32) for _ in range(7)]
        for b in range(cols // 8):
            window = [pad_ref[t, r, pl.ds(b * 8 + 5 + j, 8), :] for r in range(rows + 6)]
            grad = [grad_ref[t, p, b * 8 : b * 8 + 8, :] for p in range(rows)]
            for i in range(7):
                for p in range(rows):
                    acc[i] = acc[i] + window[p + i] * grad[p]
        for i in range(7):
            out_ref[t, j, i] = acc[i]
        return carry

    lax.fori_loop(0, 14, step, 0)


def write_chunks(chunk_ref, base, part):
    for n in range(part.shape[0] // BIG_ROWS):
        chunk_ref[base + n, 0:BIG_ROWS, :] = part[n * BIG_ROWS : (n + 1) * BIG_ROWS]


def block_kernel(
    odd_ref, own_ref, near_rows_ref, far_rows_ref, near_cols_ref, far_cols_ref, mask_ref, masked_ref, k_ref, dw_bias_ref,
    gain_ref, bias_ref, w_in_ref, b_in_ref, w_out_ref, b_out_ref, scale_ref,
    out_ref, grad_ref, chunk_ref,
    pad_ref, depth_ref, terms_ref, small_ref,
):
    rows, cols, channels = own_ref.shape
    cells = rows * cols
    hidden = w_in_ref.shape[1]
    halves = channels // LANES
    fill_padded(odd_ref, pad_ref, own_ref, near_rows_ref, far_rows_ref, near_cols_ref, far_cols_ref)
    convolve(pad_ref, k_ref, depth_ref, rows, cols, False)
    depth = jnp.concatenate([depth_ref[t].reshape(cells, LANES) for t in range(2)], axis=1)
    depth = depth + dw_bias_ref[...]
    center = depth - jnp.mean(depth, axis=-1, keepdims=True)
    inv_std = lax.rsqrt(jnp.mean(center * center, axis=-1, keepdims=True) + 1e-6)
    norm_hat = center * inv_std
    normed = (norm_hat * gain_ref[...] + bias_ref[...]).astype(BF16)
    masked = masked_ref[...].astype(F32)
    grad_branch = (masked * scale_ref[...]).astype(BF16)
    branch = jnp.zeros((cells, channels), F32)
    grad_norm = jnp.zeros((cells, channels), F32)
    root = math.sqrt(2.0 / math.pi)
    b_in_sums = []
    width = channels
    for h in range(hidden // width):
        at = slice(h * width, (h + 1) * width)
        w_in = w_in_ref[:, at]
        w_out = w_out_ref[at, :]
        pre = dot(normed, w_in, 1, 0) + b_in_ref[:, at]
        square = pre * pre
        bent = jnp.tanh(root * pre * (1.0 + 0.044715 * square))
        half = 0.5 * (1.0 + bent)
        act = (pre * half).astype(BF16)
        slope = half + (0.5 * root) * pre * (1.0 - bent * bent) * (1.0 + (3 * 0.044715) * square)
        grad_pre = (dot(grad_branch, w_out, 1, 1) * slope).astype(BF16)
        branch = branch + dot(act, w_out, 1, 0)
        grad_norm = grad_norm + dot(grad_pre, w_in, 1, 1)
        g_in = dot(normed, grad_pre, 0, 0).astype(BF16)
        g_out = dot(act, grad_branch, 0, 0).astype(BF16)
        for t in range(width // LANES):
            base = (h * (width // LANES) + t) * (channels // BIG_ROWS)
            write_chunks(chunk_ref, base, g_in[:, t * LANES : (t + 1) * LANES])
        for t in range(halves):
            base = (hidden * halves + t * hidden + h * width) // BIG_ROWS
            write_chunks(chunk_ref, base, g_out[:, t * LANES : (t + 1) * LANES])
        b_in_sums.append(jnp.sum(grad_pre.astype(F32), axis=0, keepdims=True))
    branch = branch + b_out_ref[...]
    mask = mask_ref[...].astype(F32)
    own = own_ref[...].reshape(cells, channels).astype(F32)
    out_ref[...] = (own + mask * scale_ref[...] * branch).astype(BF16).reshape(rows, cols, channels)
    scaled = grad_norm * gain_ref[...]
    mean_u = jnp.mean(scaled, axis=-1, keepdims=True)
    mean_un = jnp.mean(scaled * norm_hat, axis=-1, keepdims=True)
    grad_depth = (inv_std * (scaled - mean_u - norm_hat * mean_un)).astype(BF16)
    grad_ref[...] = grad_depth.reshape(rows, cols, channels)
    grad_float = grad_depth.astype(F32)
    for t in range(2):
        depth_ref[t] = grad_float[:, t * LANES : (t + 1) * LANES].reshape(rows, cols, LANES)
    kernel_sums(pad_ref, depth_ref, terms_ref, rows, cols)
    singles = b_in_sums + [
        jnp.sum(grad_float, axis=0, keepdims=True),
        jnp.sum(grad_norm * norm_hat, axis=0, keepdims=True),
        jnp.sum(grad_norm, axis=0, keepdims=True),
        jnp.sum(grad_branch.astype(F32), axis=0, keepdims=True),
        jnp.sum(masked * branch, axis=0, keepdims=True),
    ]
    for t in range(2):
        ln = slice(t * LANES, (t + 1) * LANES)
        small_ref[t, 0:49, :] = jnp.sum(terms_ref[t].reshape(49, 8, LANES), axis=1)
        for n, single in enumerate(singles):
            small_ref[t, 49 + n : 50 + n, :] = single[:, ln]
        small_ref[t, 49 + len(singles) :, :] = jnp.zeros((64 - 49 - len(singles), LANES), F32)
    chunks = chunk_ref.shape[0]
    for c in range(chunks):
        n = c % (chunks // 2)
        if n < 16:
            piece = small_ref[n // 8, (n % 8) * 8 : (n % 8) * 8 + 8, :].astype(BF16)
        else:
            piece = jnp.zeros((8, LANES), BF16)
        chunk_ref[c, BIG_ROWS:, :] = piece


def state_kernel(
    odd_ref, own_ref, near_rows_ref, far_rows_ref, near_cols_ref, far_cols_ref, cot_ref, k_ref, out_ref, pad_ref, sum_ref
):
    rows, cols, _ = own_ref.shape
    fill_padded(odd_ref, pad_ref, own_ref, near_rows_ref, far_rows_ref, near_cols_ref, far_cols_ref)
    convolve(pad_ref, k_ref, sum_ref, rows, cols, True)
    for t in range(2):
        ln = slice(t * LANES, (t + 1) * LANES)
        out_ref[:, :, ln] = (cot_ref[:, :, ln].astype(F32) + sum_ref[t]).astype(BF16)


def unpack_kernel(
    factor, core_ref, mine_ref, other_ref, k_ref, one_ref, two_ref, three_ref, w_in_ref, b_in_ref, w_out_ref, four_ref,
    five_ref, small_ref,
):
    channels, hidden = w_in_ref.shape

    def rows_of(ref, at, size):
        part = ref[at // BIG_ROWS : (at + size) // BIG_ROWS, 0:BIG_ROWS, :]
        return part.astype(F32).reshape(size, LANES) * factor

    def write(first_ref, second_ref):
        for t in range(hidden // LANES):
            w_in_ref[:, t * LANES : (t + 1) * LANES] = rows_of(first_ref, t * channels, channels)
        for t in range(channels // LANES):
            w_out_ref[:, t * LANES : (t + 1) * LANES] = rows_of(second_ref, t * hidden, hidden)

    @pl.when(core_ref[0] == 0)
    def _():
        write(mine_ref, other_ref)

    @pl.when(core_ref[0] != 0)
    def _():
        write(other_ref, mine_ref)

    small_ref[...] = mine_ref[0:16, BIG_ROWS:, :].astype(F32).reshape(128, LANES) * factor
    blocks = hidden // channels
    for t in range(2):
        ln = slice(t * LANES, (t + 1) * LANES)
        for j in range(7):
            for i in range(7):
                at = t * 64 + j * 7 + i
                k_ref[i, j : j + 1, ln] = small_ref[at : at + 1, :]
        at = t * 64 + 49
        for n in range(blocks):
            part = slice(n * channels + t * LANES, n * channels + (t + 1) * LANES)
            b_in_ref[:, part] = small_ref[at + n : at + n + 1, :]
        for n, ref in enumerate((one_ref, two_ref, three_ref, four_ref, five_ref)):
            ref[:, ln] = small_ref[at + blocks + n : at + blocks + n + 1, :]


def groups_along(first_core, second_core):
    index = np.arange(math.prod(SIZES.values())).reshape(tuple(SIZES.values()))
    groups = []
    for core, axes in enumerate((first_core, second_core)):
        mine = index.take(core, axis=EVERY.index("core"))
        names = [name for name in EVERY if name != "core"]
        order = [name for name in names if name not in axes] + list(axes)
        size = math.prod(SIZES[name] for name in axes)
        groups += mine.transpose([names.index(name) for name in order]).reshape(-1, size).tolist()
    return groups


PLANE = groups_along(("x", "z"), ("x", "y_hi", "y_lo"))
COLUMN = groups_along(("y_hi", "y_lo"), ("z",))


def exchange(value, groups):
    return lax.all_to_all(value, EVERY, 0, 0, axis_index_groups=groups)


def swaps(axis, wrap):
    size = lax.axis_size(axis)
    near = [(i, i ^ 1) for i in range(size)]
    far = []
    for i in range(1, size if wrap else size - 1, 2):
        far += [(i, (i + 1) % size), ((i + 1) % size, i)]
    return near, far


def swap_rows(field, odd):
    rows = field.shape[0]
    near, far = swaps(LAT, False)
    first, last = field[:3], field[rows - 3 :]
    far_rows = lax.ppermute(jnp.where(odd, last, first), LAT, far)
    near_rows = lax.ppermute(jnp.where(odd, first, last), LAT, near)
    return near_rows, far_rows


def swap_cols(field, near_rows, far_rows, odd_lat, odd_lon):
    cols = field.shape[1]
    near, far = swaps(LON, True)

    def strip(at):
        part = slice(at, at + 3)
        before = jnp.where(odd_lat, near_rows[:, part], far_rows[:, part])
        after = jnp.where(odd_lat, far_rows[:, part], near_rows[:, part])
        return jnp.concatenate([before, field[:, part], after], axis=0)

    first, last = strip(0), strip(cols - 3)
    far_cols = lax.ppermute(jnp.where(odd_lon, last, first), LON, far)
    near_cols = lax.ppermute(jnp.where(odd_lon, first, last), LON, near)
    return near_cols, far_cols


def local(
    ocean_state, land_sea, cotangent, dw_kernel, dw_bias, ln_gain, ln_bias, w_in, b_in, w_out, b_out, layer_scale
):
    _, rows, cols, channels = ocean_state.shape
    cells = rows * cols
    hidden = w_in.shape[1]
    plane, column = len(PLANE[0]), len(COLUMN[0])
    core = lax.axis_index("core")
    own = ocean_state[0]
    cot = cotangent[0]
    odd_lat = lax.axis_index("z") & 1
    odd = jnp.stack([odd_lat, core]).astype(jnp.int32)
    odd_lat, odd_lon = odd_lat == 1, core == 1
    near_rows, far_rows = swap_rows(own, odd_lat)
    near_cols, far_cols = swap_cols(own, near_rows, far_rows, odd_lat, odd_lon)
    mask = jnp.broadcast_to(land_sea[0].astype(BF16)[..., None], cot.shape)
    masked = mask * cot
    pad = pltpu.VMEM((2, rows + 6, cols + 16, LANES), F32)
    cells_scratch = pltpu.VMEM((2, rows, cols, LANES), F32)
    smem, vmem = pl.BlockSpec(memory_space=pltpu.SMEM), pl.BlockSpec(memory_space=pltpu.VMEM)
    params = pltpu.CompilerParams(vmem_limit_bytes=VMEM_BYTES)
    output, grad_depth, chunks = pl.pallas_call(
        block_kernel,
        out_shape=(
            jax.ShapeDtypeStruct((rows, cols, channels), BF16),
            jax.ShapeDtypeStruct((rows, cols, channels), BF16),
            jax.ShapeDtypeStruct((2 * plane, CHUNK_ROWS, LANES), BF16),
        ),
        in_specs=[smem] + [vmem] * 16,
        scratch_shapes=[
            pad,
            cells_scratch,
            pltpu.VMEM((2, 7, 7, 8, LANES), F32),
            pltpu.VMEM((2, 64, LANES), F32),
        ],
        compiler_params=params,
        cost_estimate=pl.CostEstimate(flops=1300000000, transcendentals=400000, bytes_accessed=6000000),
        name="block",
    )(
        odd, own, near_rows, far_rows, near_cols, far_cols, mask.reshape(cells, channels), masked.reshape(cells, channels), dw_kernel,
        dw_bias[None], ln_gain[None], ln_bias[None], w_in, b_in[None], w_out, b_out[None], layer_scale[None],
    )
    rows_sent = swap_rows(grad_depth, odd_lat)
    pair = lax.all_to_all(chunks.reshape(2, plane, CHUNK_ROWS, LANES), "core", 0, 0)
    value = (pair[0].astype(F32) + pair[1].astype(F32)).astype(BF16)
    value = exchange(value, PLANE)
    value = jnp.sum(value.astype(F32), axis=0).astype(BF16)
    value, rows_sent = lax.optimization_barrier((value, rows_sent))
    value = exchange(jnp.broadcast_to(value[None], (column,) + value.shape), COLUMN)
    value = jnp.sum(value.astype(F32), axis=0).astype(BF16)
    value = exchange(jnp.broadcast_to(value[None], (plane,) + value.shape), PLANE)
    cols_sent = swap_cols(grad_depth, *rows_sent, odd_lat, odd_lon)
    grad_state = pl.pallas_call(
        state_kernel,
        out_shape=jax.ShapeDtypeStruct((rows, cols, channels), BF16),
        in_specs=[smem] + [vmem] * 7,
        scratch_shapes=[pad, cells_scratch],
        compiler_params=params,
        cost_estimate=pl.CostEstimate(flops=10000000, transcendentals=0, bytes_accessed=3000000),
        name="state",
    )(odd, grad_depth, *rows_sent, *cols_sent, cot, dw_kernel)
    value, grad_state = lax.optimization_barrier((value, grad_state))
    other = lax.ppermute(value, "core", [(0, 1), (1, 0)])
    total_cells = cells * lax.axis_size(LON) * lax.axis_size(LAT)
    factor = 1.0 / math.sqrt(total_cells)
    single = jax.ShapeDtypeStruct((1, channels), F32)
    sums = pl.pallas_call(
        functools.partial(unpack_kernel, factor),
        out_shape=(
            jax.ShapeDtypeStruct(dw_kernel.shape, F32),
            single,
            single,
            single,
            jax.ShapeDtypeStruct((channels, hidden), F32),
            jax.ShapeDtypeStruct((1, hidden), F32),
            jax.ShapeDtypeStruct((hidden, channels), F32),
            single,
            single,
        ),
        in_specs=[smem, vmem, vmem],
        scratch_shapes=[pltpu.VMEM((128, LANES), F32)],
        compiler_params=params,
        name="unpack",
    )(core.astype(jnp.int32).reshape(1), value, other)
    sums = [part[0] if part.shape[0] == 1 else part for part in sums]
    return (output[None], grad_state[None], *sums)


def solution(mesh):
    mesh = Mesh(mesh.devices.reshape(tuple(SIZES.values())), EVERY)
    field = P(None, LAT, LON, None)
    in_specs = (field, P(None, LAT, LON), field) + (P(),) * 9
    out_specs = (field, field) + (P(),) * 9
    return jax.shard_map(local, mesh=mesh, in_specs=in_specs, out_specs=out_specs, check_vma=False)
```

```python
import functools
import math

import jax
import jax.numpy as jnp
import numpy as np
from jax import lax
from jax.experimental import pallas as pl
from jax.experimental.pallas import tpu as pltpu
from jax.sharding import Mesh, PartitionSpec as P

LON = ("y_lo", "core")
LAT = ("x", "y_hi", "z")
SIZES = {"y_lo": 4, "core": 2, "x": 4, "y_hi": 2, "z": 8}
EVERY = tuple(SIZES)
BIG_ROWS = 64
CHUNK_ROWS = 72
LANES = 128
VMEM_BYTES = 32 << 20
F32 = jnp.float32
BF16 = jnp.bfloat16


def dot(a, b, ca, cb):
    return lax.dot_general(a, b, (((ca,), (cb,)), ((), ())), preferred_element_type=F32)


def fill_padded(odd_ref, pad_ref, own_ref, near_rows_ref, far_rows_ref, near_cols_ref, far_cols_ref):
    rows, cols, _ = own_ref.shape
    low = rows + 3
    near_at = jnp.where(odd_ref[0] == 1, 0, low)
    far_at = low - near_at
    for t in range(2):
        ln = slice(t * LANES, (t + 1) * LANES)
        pad_ref[t, 3 : 3 + rows, 8 : 8 + cols] = own_ref[:, :, ln].astype(F32)
        pad_ref[t, pl.ds(near_at, 3), 8 : 8 + cols] = near_rows_ref[:, :, ln].astype(F32)
        pad_ref[t, pl.ds(far_at, 3), 8 : 8 + cols] = far_rows_ref[:, :, ln].astype(F32)

    def place(left_ref, right_ref):
        for t in range(2):
            ln = slice(t * LANES, (t + 1) * LANES)
            pad_ref[t, :, 5:8] = left_ref[:, :, ln].astype(F32)
            pad_ref[t, :, 8 + cols : 11 + cols] = right_ref[:, :, ln].astype(F32)

    @pl.when(odd_ref[1] == 0)
    def _():
        place(far_cols_ref, near_cols_ref)

    @pl.when(odd_ref[1] != 0)
    def _():
        place(near_cols_ref, far_cols_ref)


def convolve(pad_ref, k_ref, out_ref, rows, cols, flip):
    for t in range(2):
        ln = slice(t * LANES, (t + 1) * LANES)

        def step(n, carry, t=t, ln=ln):
            at = pl.multiple_of(n * 8, 8)
            acc = [jnp.zeros((8, LANES), F32) for _ in range(rows)]
            for j in range(7):
                window = [pad_ref[t, r, pl.ds(at + 5 + j, 8), :] for r in range(rows + 6)]
                for i in range(7):
                    row, col = (6 - i, 6 - j) if flip else (i, j)
                    weight = k_ref[row, col : col + 1, ln]
                    for p in range(rows):
                        acc[p] = acc[p] + window[p + i] * weight
            for p in range(rows):
                out_ref[t, p, pl.ds(at, 8), :] = acc[p]
            return carry

        lax.fori_loop(0, cols // 8, step, 0)


def kernel_sums(pad_ref, grad_ref, out_ref, rows, cols):
    def step(n, carry):
        t, j = n // 7, n % 7
        acc = [jnp.zeros((8, LANES), F32) for _ in range(7)]
        for b in range(cols // 8):
            window = [pad_ref[t, r, pl.ds(b * 8 + 5 + j, 8), :] for r in range(rows + 6)]
            grad = [grad_ref[t, p, b * 8 : b * 8 + 8, :] for p in range(rows)]
            for i in range(7):
                for p in range(rows):
                    acc[i] = acc[i] + window[p + i] * grad[p]
        for i in range(7):
            out_ref[t, j, i] = acc[i]
        return carry

    lax.fori_loop(0, 14, step, 0)


def write_chunks(chunk_ref, base, part):
    for n in range(part.shape[0] // BIG_ROWS):
        chunk_ref[base + n, 0:BIG_ROWS, :] = part[n * BIG_ROWS : (n + 1) * BIG_ROWS]


def block_kernel(
    odd_ref, own_ref, near_rows_ref, far_rows_ref, near_cols_ref, far_cols_ref, mask_ref, masked_ref, k_ref, dw_bias_ref,
    gain_ref, bias_ref, w_in_ref, b_in_ref, w_out_ref, b_out_ref, scale_ref,
    out_ref, grad_ref, chunk_ref,
    pad_ref, depth_ref, terms_ref, small_ref,
):
    rows, cols, channels = own_ref.shape
    cells = rows * cols
    hidden = w_in_ref.shape[1]
    halves = channels // LANES
    fill_padded(odd_ref, pad_ref, own_ref, near_rows_ref, far_rows_ref, near_cols_ref, far_cols_ref)
    convolve(pad_ref, k_ref, depth_ref, rows, cols, False)
    depth = jnp.concatenate([depth_ref[t].reshape(cells, LANES) for t in range(2)], axis=1)
    depth = depth + dw_bias_ref[...]
    center = depth - jnp.mean(depth, axis=-1, keepdims=True)
    inv_std = lax.rsqrt(jnp.mean(center * center, axis=-1, keepdims=True) + 1e-6)
    norm_hat = center * inv_std
    normed = (norm_hat * gain_ref[...] + bias_ref[...]).astype(BF16)
    masked = masked_ref[...].astype(F32)
    grad_branch = (masked * scale_ref[...]).astype(BF16)
    branch = jnp.zeros((cells, channels), F32)
    grad_norm = jnp.zeros((cells, channels), F32)
    root = math.sqrt(2.0 / math.pi)
    b_in_sums = []
    width = channels
    for h in range(hidden // width):
        at = slice(h * width, (h + 1) * width)
        w_in = w_in_ref[:, at]
        w_out = w_out_ref[at, :]
        pre = dot(normed, w_in, 1, 0) + b_in_ref[:, at]
        square = pre * pre
        bent = jnp.tanh(root * pre * (1.0 + 0.044715 * square))
        half = 0.5 * (1.0 + bent)
        act = (pre * half).astype(BF16)
        slope = half + (0.5 * root) * pre * (1.0 - bent * bent) * (1.0 + (3 * 0.044715) * square)
        grad_pre = (dot(grad_branch, w_out, 1, 1) * slope).astype(BF16)
        branch = branch + dot(act, w_out, 1, 0)
        grad_norm = grad_norm + dot(grad_pre, w_in, 1, 1)
        g_in = dot(normed, grad_pre, 0, 0).astype(BF16)
        g_out = dot(act, grad_branch, 0, 0).astype(BF16)
        for t in range(width // LANES):
            base = (h * (width // LANES) + t) * (channels // BIG_ROWS)
            write_chunks(chunk_ref, base, g_in[:, t * LANES : (t + 1) * LANES])
        for t in range(halves):
            base = (hidden * halves + t * hidden + h * width) // BIG_ROWS
            write_chunks(chunk_ref, base, g_out[:, t * LANES : (t + 1) * LANES])
        b_in_sums.append(jnp.sum(grad_pre.astype(F32), axis=0, keepdims=True))
    branch = branch + b_out_ref[...]
    mask = mask_ref[...].astype(F32)
    own = own_ref[...].reshape(cells, channels).astype(F32)
    out_ref[...] = (own + mask * scale_ref[...] * branch).astype(BF16).reshape(rows, cols, channels)
    scaled = grad_norm * gain_ref[...]
    mean_u = jnp.mean(scaled, axis=-1, keepdims=True)
    mean_un = jnp.mean(scaled * norm_hat, axis=-1, keepdims=True)
    grad_depth = (inv_std * (scaled - mean_u - norm_hat * mean_un)).astype(BF16)
    grad_ref[...] = grad_depth.reshape(rows, cols, channels)
    grad_float = grad_depth.astype(F32)
    for t in range(2):
        depth_ref[t] = grad_float[:, t * LANES : (t + 1) * LANES].reshape(rows, cols, LANES)
    kernel_sums(pad_ref, depth_ref, terms_ref, rows, cols)
    singles = b_in_sums + [
        jnp.sum(grad_float, axis=0, keepdims=True),
        jnp.sum(grad_norm * norm_hat, axis=0, keepdims=True),
        jnp.sum(grad_norm, axis=0, keepdims=True),
        jnp.sum(grad_branch.astype(F32), axis=0, keepdims=True),
        jnp.sum(masked * branch, axis=0, keepdims=True),
    ]
    for t in range(2):
        ln = slice(t * LANES, (t + 1) * LANES)
        small_ref[t, 0:49, :] = jnp.sum(terms_ref[t].reshape(49, 8, LANES), axis=1)
        for n, single in enumerate(singles):
            small_ref[t, 49 + n : 50 + n, :] = single[:, ln]
        small_ref[t, 49 + len(singles) :, :] = jnp.zeros((64 - 49 - len(singles), LANES), F32)
    chunks = chunk_ref.shape[0]
    for c in range(chunks):
        n = c % (chunks // 2)
        if n < 16:
            piece = small_ref[n // 8, (n % 8) * 8 : (n % 8) * 8 + 8, :].astype(BF16)
        else:
            piece = jnp.zeros((8, LANES), BF16)
        chunk_ref[c, BIG_ROWS:, :] = piece


def state_kernel(
    odd_ref, own_ref, near_rows_ref, far_rows_ref, near_cols_ref, far_cols_ref, cot_ref, k_ref, out_ref, pad_ref, sum_ref
):
    rows, cols, _ = own_ref.shape
    fill_padded(odd_ref, pad_ref, own_ref, near_rows_ref, far_rows_ref, near_cols_ref, far_cols_ref)
    convolve(pad_ref, k_ref, sum_ref, rows, cols, True)
    for t in range(2):
        ln = slice(t * LANES, (t + 1) * LANES)
        out_ref[:, :, ln] = (cot_ref[:, :, ln].astype(F32) + sum_ref[t]).astype(BF16)


def unpack_kernel(
    factor, core_ref, mine_ref, other_ref, k_ref, one_ref, two_ref, three_ref, w_in_ref, b_in_ref, w_out_ref, four_ref,
    five_ref, small_ref,
):
    channels, hidden = w_in_ref.shape

    def rows_of(ref, at, size):
        part = ref[at // BIG_ROWS : (at + size) // BIG_ROWS, 0:BIG_ROWS, :]
        return part.astype(F32).reshape(size, LANES) * factor

    def write(first_ref, second_ref):
        for t in range(hidden // LANES):
            w_in_ref[:, t * LANES : (t + 1) * LANES] = rows_of(first_ref, t * channels, channels)
        for t in range(channels // LANES):
            w_out_ref[:, t * LANES : (t + 1) * LANES] = rows_of(second_ref, t * hidden, hidden)

    @pl.when(core_ref[0] == 0)
    def _():
        write(mine_ref, other_ref)

    @pl.when(core_ref[0] != 0)
    def _():
        write(other_ref, mine_ref)

    small_ref[...] = mine_ref[0:16, BIG_ROWS:, :].astype(F32).reshape(128, LANES) * factor
    blocks = hidden // channels
    for t in range(2):
        ln = slice(t * LANES, (t + 1) * LANES)
        for j in range(7):
            for i in range(7):
                at = t * 64 + j * 7 + i
                k_ref[i, j : j + 1, ln] = small_ref[at : at + 1, :]
        at = t * 64 + 49
        for n in range(blocks):
            part = slice(n * channels + t * LANES, n * channels + (t + 1) * LANES)
            b_in_ref[:, part] = small_ref[at + n : at + n + 1, :]
        for n, ref in enumerate((one_ref, two_ref, three_ref, four_ref, five_ref)):
            ref[:, ln] = small_ref[at + blocks + n : at + blocks + n + 1, :]


def groups_along(first_core, second_core):
    index = np.arange(math.prod(SIZES.values())).reshape(tuple(SIZES.values()))
    groups = []
    for core, axes in enumerate((first_core, second_core)):
        mine = index.take(core, axis=EVERY.index("core"))
        names = [name for name in EVERY if name != "core"]
        order = [name for name in names if name not in axes] + list(axes)
        size = math.prod(SIZES[name] for name in axes)
        groups += mine.transpose([names.index(name) for name in order]).reshape(-1, size).tolist()
    return groups


PLANE = groups_along(("x", "z"), ("x", "y_hi", "y_lo"))
COLUMN = groups_along(("y_hi", "y_lo"), ("z",))


def exchange(value, groups):
    return lax.all_to_all(value, EVERY, 0, 0, axis_index_groups=groups)


def swaps(axis, wrap):
    size = lax.axis_size(axis)
    near = [(i, i ^ 1) for i in range(size)]
    far = []
    for i in range(1, size if wrap else size - 1, 2):
        far += [(i, (i + 1) % size), ((i + 1) % size, i)]
    return near, far


def swap_rows(field, odd):
    rows = field.shape[0]
    near, far = swaps(LAT, False)
    first, last = field[:3], field[rows - 3 :]
    far_rows = lax.ppermute(jnp.where(odd, last, first), LAT, far)
    near_rows = lax.ppermute(jnp.where(odd, first, last), LAT, near)
    return near_rows, far_rows


def swap_cols(field, near_rows, far_rows, odd_lat, odd_lon):
    cols = field.shape[1]
    near, far = swaps(LON, True)

    def strip(at):
        part = slice(at, at + 3)
        before = jnp.where(odd_lat, near_rows[:, part], far_rows[:, part])
        after = jnp.where(odd_lat, far_rows[:, part], near_rows[:, part])
        return jnp.concatenate([before, field[:, part], after], axis=0)

    first, last = strip(0), strip(cols - 3)
    far_cols = lax.ppermute(jnp.where(odd_lon, last, first), LON, far)
    near_cols = lax.ppermute(jnp.where(odd_lon, first, last), LON, near)
    return near_cols, far_cols


def local(
    ocean_state, land_sea, cotangent, dw_kernel, dw_bias, ln_gain, ln_bias, w_in, b_in, w_out, b_out, layer_scale
):
    _, rows, cols, channels = ocean_state.shape
    cells = rows * cols
    hidden = w_in.shape[1]
    plane, column = len(PLANE[0]), len(COLUMN[0])
    core = lax.axis_index("core")
    own = ocean_state[0]
    cot = cotangent[0]
    odd_lat = lax.axis_index("z") & 1
    odd = jnp.stack([odd_lat, core]).astype(jnp.int32)
    odd_lat, odd_lon = odd_lat == 1, core == 1
    near_rows, far_rows = swap_rows(own, odd_lat)
    near_cols, far_cols = swap_cols(own, near_rows, far_rows, odd_lat, odd_lon)
    mask = jnp.broadcast_to(land_sea[0].astype(BF16)[..., None], cot.shape)
    masked = mask * cot
    pad = pltpu.VMEM((2, rows + 6, cols + 16, LANES), F32)
    cells_scratch = pltpu.VMEM((2, rows, cols, LANES), F32)
    smem, vmem = pl.BlockSpec(memory_space=pltpu.SMEM), pl.BlockSpec(memory_space=pltpu.VMEM)
    params = pltpu.CompilerParams(vmem_limit_bytes=VMEM_BYTES)
    output, grad_depth, chunks = pl.pallas_call(
        block_kernel,
        out_shape=(
            jax.ShapeDtypeStruct((rows, cols, channels), BF16),
            jax.ShapeDtypeStruct((rows, cols, channels), BF16),
            jax.ShapeDtypeStruct((2 * plane, CHUNK_ROWS, LANES), BF16),
        ),
        in_specs=[smem] + [vmem] * 16,
        scratch_shapes=[
            pad,
            cells_scratch,
            pltpu.VMEM((2, 7, 7, 8, LANES), F32),
            pltpu.VMEM((2, 64, LANES), F32),
        ],
        compiler_params=params,
        cost_estimate=pl.CostEstimate(flops=1300000000, transcendentals=400000, bytes_accessed=6000000),
        name="block",
    )(
        odd, own, near_rows, far_rows, near_cols, far_cols, mask.reshape(cells, channels), masked.reshape(cells, channels), dw_kernel,
        dw_bias[None], ln_gain[None], ln_bias[None], w_in, b_in[None], w_out, b_out[None], layer_scale[None],
    )
    rows_sent = swap_rows(grad_depth, odd_lat)
    pair = lax.all_to_all(chunks.reshape(2, plane, CHUNK_ROWS, LANES), "core", 0, 0)
    value = (pair[0].astype(F32) + pair[1].astype(F32)).astype(BF16)
    value = exchange(value, PLANE)
    value = jnp.sum(value.astype(F32), axis=0).astype(BF16)
    value = exchange(jnp.broadcast_to(value[None], (column,) + value.shape), COLUMN)
    value = jnp.sum(value.astype(F32), axis=0).astype(BF16)
    value, rows_sent = lax.optimization_barrier((value, rows_sent))
    value = exchange(jnp.broadcast_to(value[None], (plane,) + value.shape), PLANE)
    cols_sent = swap_cols(grad_depth, *rows_sent, odd_lat, odd_lon)
    value, cols_sent = lax.optimization_barrier((value, cols_sent))
    grad_state = pl.pallas_call(
        state_kernel,
        out_shape=jax.ShapeDtypeStruct((rows, cols, channels), BF16),
        in_specs=[smem] + [vmem] * 7,
        scratch_shapes=[pad, cells_scratch],
        compiler_params=params,
        cost_estimate=pl.CostEstimate(flops=10000000, transcendentals=0, bytes_accessed=3000000),
        name="state",
    )(odd, grad_depth, *rows_sent, *cols_sent, cot, dw_kernel)
    other = lax.ppermute(value, "core", [(0, 1), (1, 0)])
    total_cells = cells * lax.axis_size(LON) * lax.axis_size(LAT)
    factor = 1.0 / math.sqrt(total_cells)
    single = jax.ShapeDtypeStruct((1, channels), F32)
    sums = pl.pallas_call(
        functools.partial(unpack_kernel, factor),
        out_shape=(
            jax.ShapeDtypeStruct(dw_kernel.shape, F32),
            single,
            single,
            single,
            jax.ShapeDtypeStruct((channels, hidden), F32),
            jax.ShapeDtypeStruct((1, hidden), F32),
            jax.ShapeDtypeStruct((hidden, channels), F32),
            single,
            single,
        ),
        in_specs=[smem, vmem, vmem],
        scratch_shapes=[pltpu.VMEM((128, LANES), F32)],
        compiler_params=params,
        name="unpack",
    )(core.astype(jnp.int32).reshape(1), value, other)
    sums = [part[0] if part.shape[0] == 1 else part for part in sums]
    return (output[None], grad_state[None], *sums)


def solution(mesh):
    mesh = Mesh(mesh.devices.reshape(tuple(SIZES.values())), EVERY)
    field = P(None, LAT, LON, None)
    in_specs = (field, P(None, LAT, LON), field) + (P(),) * 9
    out_specs = (field, field) + (P(),) * 9
    return jax.shard_map(local, mesh=mesh, in_specs=in_specs, out_specs=out_specs, check_vma=False)
```

```python
import functools
import math

import jax
import jax.numpy as jnp
import numpy as np
from jax import lax
from jax.experimental import pallas as pl
from jax.experimental.pallas import tpu as pltpu
from jax.sharding import Mesh, PartitionSpec as P

LON = ("y_lo", "core")
LAT = ("x", "y_hi", "z")
SIZES = {"y_lo": 4, "core": 2, "x": 4, "y_hi": 2, "z": 8}
EVERY = tuple(SIZES)
BIG_ROWS = 64
CHUNK_ROWS = 72
LANES = 128
VMEM_BYTES = 32 << 20
F32 = jnp.float32
BF16 = jnp.bfloat16


def dot(a, b, ca, cb):
    return lax.dot_general(a, b, (((ca,), (cb,)), ((), ())), preferred_element_type=F32)


def fill_padded(odd_ref, pad_ref, own_ref, near_rows_ref, far_rows_ref, near_cols_ref, far_cols_ref):
    rows, cols, _ = own_ref.shape
    low = rows + 3
    near_at = jnp.where(odd_ref[0] == 1, 0, low)
    far_at = low - near_at
    for t in range(2):
        ln = slice(t * LANES, (t + 1) * LANES)
        pad_ref[t, 3 : 3 + rows, 8 : 8 + cols] = own_ref[:, :, ln].astype(F32)
        pad_ref[t, pl.ds(near_at, 3), 8 : 8 + cols] = near_rows_ref[:, :, ln].astype(F32)
        pad_ref[t, pl.ds(far_at, 3), 8 : 8 + cols] = far_rows_ref[:, :, ln].astype(F32)

    def place(left_ref, right_ref):
        for t in range(2):
            ln = slice(t * LANES, (t + 1) * LANES)
            pad_ref[t, :, 5:8] = left_ref[:, :, ln].astype(F32)
            pad_ref[t, :, 8 + cols : 11 + cols] = right_ref[:, :, ln].astype(F32)

    @pl.when(odd_ref[1] == 0)
    def _():
        place(far_cols_ref, near_cols_ref)

    @pl.when(odd_ref[1] != 0)
    def _():
        place(near_cols_ref, far_cols_ref)


def convolve(pad_ref, k_ref, out_ref, rows, cols, flip):
    for t in range(2):
        ln = slice(t * LANES, (t + 1) * LANES)

        def step(n, carry, t=t, ln=ln):
            at = pl.multiple_of(n * 8, 8)
            acc = [jnp.zeros((8, LANES), F32) for _ in range(rows)]
            for j in range(7):
                window = [pad_ref[t, r, pl.ds(at + 5 + j, 8), :] for r in range(rows + 6)]
                for i in range(7):
                    row, col = (6 - i, 6 - j) if flip else (i, j)
                    weight = k_ref[row, col : col + 1, ln]
                    for p in range(rows):
                        acc[p] = acc[p] + window[p + i] * weight
            for p in range(rows):
                out_ref[t, p, pl.ds(at, 8), :] = acc[p]
            return carry

        lax.fori_loop(0, cols // 8, step, 0)


def kernel_sums(pad_ref, grad_ref, out_ref, rows, cols):
    def step(n, carry):
        t, j = n // 7, n % 7
        acc = [jnp.zeros((8, LANES), F32) for _ in range(7)]
        for b in range(cols // 8):
            window = [pad_ref[t, r, pl.ds(b * 8 + 5 + j, 8), :] for r in range(rows + 6)]
            grad = [grad_ref[t, p, b * 8 : b * 8 + 8, :] for p in range(rows)]
            for i in range(7):
                for p in range(rows):
                    acc[i] = acc[i] + window[p + i] * grad[p]
        for i in range(7):
            out_ref[t, j, i] = acc[i]
        return carry

    lax.fori_loop(0, 14, step, 0)


def write_chunks(chunk_ref, base, part):
    for n in range(part.shape[0] // BIG_ROWS):
        chunk_ref[base + n, 0:BIG_ROWS, :] = part[n * BIG_ROWS : (n + 1) * BIG_ROWS]


def block_kernel(
    odd_ref, own_ref, near_rows_ref, far_rows_ref, near_cols_ref, far_cols_ref, mask_ref, masked_ref, k_ref, dw_bias_ref,
    gain_ref, bias_ref, w_in_ref, b_in_ref, w_out_ref, b_out_ref, scale_ref,
    out_ref, grad_ref, chunk_ref,
    pad_ref, depth_ref, terms_ref, small_ref,
):
    rows, cols, channels = own_ref.shape
    cells = rows * cols
    hidden = w_in_ref.shape[1]
    halves = channels // LANES
    fill_padded(odd_ref, pad_ref, own_ref, near_rows_ref, far_rows_ref, near_cols_ref, far_cols_ref)
    convolve(pad_ref, k_ref, depth_ref, rows, cols, False)
    depth = jnp.concatenate([depth_ref[t].reshape(cells, LANES) for t in range(2)], axis=1)
    depth = depth + dw_bias_ref[...]
    center = depth - jnp.mean(depth, axis=-1, keepdims=True)
    inv_std = lax.rsqrt(jnp.mean(center * center, axis=-1, keepdims=True) + 1e-6)
    norm_hat = center * inv_std
    normed = (norm_hat * gain_ref[...] + bias_ref[...]).astype(BF16)
    masked = masked_ref[...].astype(F32)
    grad_branch = (masked * scale_ref[...]).astype(BF16)
    branch = jnp.zeros((cells, channels), F32)
    grad_norm = jnp.zeros((cells, channels), F32)
    root = math.sqrt(2.0 / math.pi)
    b_in_sums = []
    width = channels
    for h in range(hidden // width):
        at = slice(h * width, (h + 1) * width)
        w_in = w_in_ref[:, at]
        w_out = w_out_ref[at, :]
        pre = dot(normed, w_in, 1, 0) + b_in_ref[:, at]
        square = pre * pre
        bent = jnp.tanh(root * pre * (1.0 + 0.044715 * square))
        half = 0.5 * (1.0 + bent)
        act = (pre * half).astype(BF16)
        slope = half + (0.5 * root) * pre * (1.0 - bent * bent) * (1.0 + (3 * 0.044715) * square)
        grad_pre = (dot(grad_branch, w_out, 1, 1) * slope).astype(BF16)
        branch = branch + dot(act, w_out, 1, 0)
        grad_norm = grad_norm + dot(grad_pre, w_in, 1, 1)
        g_in = dot(normed, grad_pre, 0, 0).astype(BF16)
        g_out = dot(act, grad_branch, 0, 0).astype(BF16)
        for t in range(width // LANES):
            base = (h * (width // LANES) + t) * (channels // BIG_ROWS)
            write_chunks(chunk_ref, base, g_in[:, t * LANES : (t + 1) * LANES])
        for t in range(halves):
            base = (hidden * halves + t * hidden + h * width) // BIG_ROWS
            write_chunks(chunk_ref, base, g_out[:, t * LANES : (t + 1) * LANES])
        b_in_sums.append(jnp.sum(grad_pre.astype(F32), axis=0, keepdims=True))
    branch = branch + b_out_ref[...]
    mask = mask_ref[...].astype(F32)
    own = own_ref[...].reshape(cells, channels).astype(F32)
    out_ref[...] = (own + mask * scale_ref[...] * branch).astype(BF16).reshape(rows, cols, channels)
    scaled = grad_norm * gain_ref[...]
    mean_u = jnp.mean(scaled, axis=-1, keepdims=True)
    mean_un = jnp.mean(scaled * norm_hat, axis=-1, keepdims=True)
    grad_depth = (inv_std * (scaled - mean_u - norm_hat * mean_un)).astype(BF16)
    grad_ref[...] = grad_depth.reshape(rows, cols, channels)
    grad_float = grad_depth.astype(F32)
    for t in range(2):
        depth_ref[t] = grad_float[:, t * LANES : (t + 1) * LANES].reshape(rows, cols, LANES)
    kernel_sums(pad_ref, depth_ref, terms_ref, rows, cols)
    singles = b_in_sums + [
        jnp.sum(grad_float, axis=0, keepdims=True),
        jnp.sum(grad_norm * norm_hat, axis=0, keepdims=True),
        jnp.sum(grad_norm, axis=0, keepdims=True),
        jnp.sum(grad_branch.astype(F32), axis=0, keepdims=True),
        jnp.sum(masked * branch, axis=0, keepdims=True),
    ]
    for t in range(2):
        ln = slice(t * LANES, (t + 1) * LANES)
        small_ref[t, 0:49, :] = jnp.sum(terms_ref[t].reshape(49, 8, LANES), axis=1)
        for n, single in enumerate(singles):
            small_ref[t, 49 + n : 50 + n, :] = single[:, ln]
        small_ref[t, 49 + len(singles) :, :] = jnp.zeros((64 - 49 - len(singles), LANES), F32)
    chunks = chunk_ref.shape[0]
    for c in range(chunks):
        n = c % (chunks // 2)
        if n < 16:
            piece = small_ref[n // 8, (n % 8) * 8 : (n % 8) * 8 + 8, :].astype(BF16)
        else:
            piece = jnp.zeros((8, LANES), BF16)
        chunk_ref[c, BIG_ROWS:, :] = piece


def state_kernel(
    odd_ref, own_ref, near_rows_ref, far_rows_ref, near_cols_ref, far_cols_ref, cot_ref, k_ref, out_ref, pad_ref, sum_ref
):
    rows, cols, _ = own_ref.shape
    fill_padded(odd_ref, pad_ref, own_ref, near_rows_ref, far_rows_ref, near_cols_ref, far_cols_ref)
    convolve(pad_ref, k_ref, sum_ref, rows, cols, True)
    for t in range(2):
        ln = slice(t * LANES, (t + 1) * LANES)
        out_ref[:, :, ln] = (cot_ref[:, :, ln].astype(F32) + sum_ref[t]).astype(BF16)


def unpack_kernel(
    factor, core_ref, mine_ref, other_ref, k_ref, one_ref, two_ref, three_ref, w_in_ref, b_in_ref, w_out_ref, four_ref,
    five_ref, small_ref,
):
    channels, hidden = w_in_ref.shape

    def rows_of(ref, at, size):
        part = ref[at // BIG_ROWS : (at + size) // BIG_ROWS, 0:BIG_ROWS, :]
        return part.astype(F32).reshape(size, LANES) * factor

    def write(first_ref, second_ref):
        for t in range(hidden // LANES):
            w_in_ref[:, t * LANES : (t + 1) * LANES] = rows_of(first_ref, t * channels, channels)
        for t in range(channels // LANES):
            w_out_ref[:, t * LANES : (t + 1) * LANES] = rows_of(second_ref, t * hidden, hidden)

    @pl.when(core_ref[0] == 0)
    def _():
        write(mine_ref, other_ref)

    @pl.when(core_ref[0] != 0)
    def _():
        write(other_ref, mine_ref)

    small_ref[...] = mine_ref[0:16, BIG_ROWS:, :].astype(F32).reshape(128, LANES) * factor
    blocks = hidden // channels
    for t in range(2):
        ln = slice(t * LANES, (t + 1) * LANES)
        for j in range(7):
            for i in range(7):
                at = t * 64 + j * 7 + i
                k_ref[i, j : j + 1, ln] = small_ref[at : at + 1, :]
        at = t * 64 + 49
        for n in range(blocks):
            part = slice(n * channels + t * LANES, n * channels + (t + 1) * LANES)
            b_in_ref[:, part] = small_ref[at + n : at + n + 1, :]
        for n, ref in enumerate((one_ref, two_ref, three_ref, four_ref, five_ref)):
            ref[:, ln] = small_ref[at + blocks + n : at + blocks + n + 1, :]


def groups_along(first_core, second_core):
    index = np.arange(math.prod(SIZES.values())).reshape(tuple(SIZES.values()))
    groups = []
    for core, axes in enumerate((first_core, second_core)):
        mine = index.take(core, axis=EVERY.index("core"))
        names = [name for name in EVERY if name != "core"]
        order = [name for name in names if name not in axes] + list(axes)
        size = math.prod(SIZES[name] for name in axes)
        groups += mine.transpose([names.index(name) for name in order]).reshape(-1, size).tolist()
    return groups


PLANE = groups_along(("x", "z"), ("x", "y_hi", "y_lo"))
COLUMN = groups_along(("y_hi", "y_lo"), ("z",))


def exchange(value, groups):
    return lax.all_to_all(value, EVERY, 0, 0, axis_index_groups=groups)


def swaps(axis, wrap):
    size = lax.axis_size(axis)
    near = [(i, i ^ 1) for i in range(size)]
    far = []
    for i in range(1, size if wrap else size - 1, 2):
        far += [(i, (i + 1) % size), ((i + 1) % size, i)]
    return near, far


def swap_rows(field, odd):
    rows = field.shape[0]
    near, far = swaps(LAT, False)
    first, last = field[:3], field[rows - 3 :]
    far_rows = lax.ppermute(jnp.where(odd, last, first), LAT, far)
    near_rows = lax.ppermute(jnp.where(odd, first, last), LAT, near)
    return near_rows, far_rows


def swap_cols(field, near_rows, far_rows, odd_lat, odd_lon):
    cols = field.shape[1]
    near, far = swaps(LON, True)

    def strip(at):
        part = slice(at, at + 3)
        before = jnp.where(odd_lat, near_rows[:, part], far_rows[:, part])
        after = jnp.where(odd_lat, far_rows[:, part], near_rows[:, part])
        return jnp.concatenate([before, field[:, part], after], axis=0)

    first, last = strip(0), strip(cols - 3)
    far_cols = lax.ppermute(jnp.where(odd_lon, last, first), LON, far)
    near_cols = lax.ppermute(jnp.where(odd_lon, first, last), LON, near)
    return near_cols, far_cols


def local(
    ocean_state, land_sea, cotangent, dw_kernel, dw_bias, ln_gain, ln_bias, w_in, b_in, w_out, b_out, layer_scale
):
    _, rows, cols, channels = ocean_state.shape
    cells = rows * cols
    hidden = w_in.shape[1]
    plane, column = len(PLANE[0]), len(COLUMN[0])
    core = lax.axis_index("core")
    own = ocean_state[0]
    cot = cotangent[0]
    odd_lat = lax.axis_index("z") & 1
    odd = jnp.stack([odd_lat, core]).astype(jnp.int32)
    odd_lat, odd_lon = odd_lat == 1, core == 1
    near_rows, far_rows = swap_rows(own, odd_lat)
    near_cols, far_cols = swap_cols(own, near_rows, far_rows, odd_lat, odd_lon)
    mask = jnp.broadcast_to(land_sea[0].astype(BF16)[..., None], cot.shape)
    masked = mask * cot
    pad = pltpu.VMEM((2, rows + 6, cols + 16, LANES), F32)
    cells_scratch = pltpu.VMEM((2, rows, cols, LANES), F32)
    smem, vmem = pl.BlockSpec(memory_space=pltpu.SMEM), pl.BlockSpec(memory_space=pltpu.VMEM)
    params = pltpu.CompilerParams(vmem_limit_bytes=VMEM_BYTES)
    output, grad_depth, chunks = pl.pallas_call(
        block_kernel,
        out_shape=(
            jax.ShapeDtypeStruct((rows, cols, channels), BF16),
            jax.ShapeDtypeStruct((rows, cols, channels), BF16),
            jax.ShapeDtypeStruct((2 * plane, CHUNK_ROWS, LANES), BF16),
        ),
        in_specs=[smem] + [vmem] * 16,
        scratch_shapes=[
            pad,
            cells_scratch,
            pltpu.VMEM((2, 7, 7, 8, LANES), F32),
            pltpu.VMEM((2, 64, LANES), F32),
        ],
        compiler_params=params,
        cost_estimate=pl.CostEstimate(flops=1300000000, transcendentals=400000, bytes_accessed=6000000),
        name="block",
    )(
        odd, own, near_rows, far_rows, near_cols, far_cols, mask.reshape(cells, channels), masked.reshape(cells, channels), dw_kernel,
        dw_bias[None], ln_gain[None], ln_bias[None], w_in, b_in[None], w_out, b_out[None], layer_scale[None],
    )
    rows_sent = swap_rows(grad_depth, odd_lat)
    pair = lax.all_to_all(chunks.reshape(2, plane, CHUNK_ROWS, LANES), "core", 0, 0)
    value = (pair[0].astype(F32) + pair[1].astype(F32)).astype(BF16)
    value = exchange(value, PLANE)
    value = jnp.sum(value.astype(F32), axis=0).astype(BF16)
    value, rows_sent = lax.optimization_barrier((value, rows_sent))
    value = exchange(jnp.broadcast_to(value[None], (column,) + value.shape), COLUMN)
    value = jnp.sum(value.astype(F32), axis=0).astype(BF16)
    value = exchange(jnp.broadcast_to(value[None], (plane,) + value.shape), PLANE)
    cols_sent = swap_cols(grad_depth, *rows_sent, odd_lat, odd_lon)
    value, cols_sent = lax.optimization_barrier((value, cols_sent))
    grad_state = pl.pallas_call(
        state_kernel,
        out_shape=jax.ShapeDtypeStruct((rows, cols, channels), BF16),
        in_specs=[smem] + [vmem] * 7,
        scratch_shapes=[pad, cells_scratch],
        compiler_params=params,
        cost_estimate=pl.CostEstimate(flops=10000000, transcendentals=0, bytes_accessed=3000000),
        name="state",
    )(odd, grad_depth, *rows_sent, *cols_sent, cot, dw_kernel)
    other = lax.ppermute(value, "core", [(0, 1), (1, 0)])
    total_cells = cells * lax.axis_size(LON) * lax.axis_size(LAT)
    factor = 1.0 / math.sqrt(total_cells)
    single = jax.ShapeDtypeStruct((1, channels), F32)
    sums = pl.pallas_call(
        functools.partial(unpack_kernel, factor),
        out_shape=(
            jax.ShapeDtypeStruct(dw_kernel.shape, F32),
            single,
            single,
            single,
            jax.ShapeDtypeStruct((channels, hidden), F32),
            jax.ShapeDtypeStruct((1, hidden), F32),
            jax.ShapeDtypeStruct((hidden, channels), F32),
            single,
            single,
        ),
        in_specs=[smem, vmem, vmem],
        scratch_shapes=[pltpu.VMEM((128, LANES), F32)],
        compiler_params=params,
        name="unpack",
    )(core.astype(jnp.int32).reshape(1), value, other)
    sums = [part[0] if part.shape[0] == 1 else part for part in sums]
    return (output[None], grad_state[None], *sums)


def solution(mesh):
    mesh = Mesh(mesh.devices.reshape(tuple(SIZES.values())), EVERY)
    field = P(None, LAT, LON, None)
    in_specs = (field, P(None, LAT, LON), field) + (P(),) * 9
    out_specs = (field, field) + (P(),) * 9
    return jax.shard_map(local, mesh=mesh, in_specs=in_specs, out_specs=out_specs, check_vma=False)
```

```python
import functools
import math

import jax
import jax.numpy as jnp
import numpy as np
from jax import lax
from jax.experimental import pallas as pl
from jax.experimental.pallas import tpu as pltpu
from jax.sharding import Mesh, PartitionSpec as P

LON = ("y_lo", "core")
LAT = ("x", "y_hi", "z")
SIZES = {"y_lo": 4, "core": 2, "x": 4, "y_hi": 2, "z": 8}
EVERY = tuple(SIZES)
BIG_ROWS = 64
CHUNK_ROWS = 72
LANES = 128
VMEM_BYTES = 32 << 20
F32 = jnp.float32
BF16 = jnp.bfloat16


def dot(a, b, ca, cb):
    return lax.dot_general(a, b, (((ca,), (cb,)), ((), ())), preferred_element_type=F32)


def fill_padded(odd_ref, pad_ref, own_ref, near_rows_ref, far_rows_ref, near_cols_ref, far_cols_ref):
    rows, cols, _ = own_ref.shape
    low = rows + 3
    near_at = jnp.where(odd_ref[0] == 1, 0, low)
    far_at = low - near_at
    for t in range(2):
        ln = slice(t * LANES, (t + 1) * LANES)
        pad_ref[t, 3 : 3 + rows, 8 : 8 + cols] = own_ref[:, :, ln].astype(F32)
        pad_ref[t, pl.ds(near_at, 3), 8 : 8 + cols] = near_rows_ref[:, :, ln].astype(F32)
        pad_ref[t, pl.ds(far_at, 3), 8 : 8 + cols] = far_rows_ref[:, :, ln].astype(F32)

    def place(left_ref, right_ref):
        for t in range(2):
            ln = slice(t * LANES, (t + 1) * LANES)
            pad_ref[t, :, 5:8] = left_ref[:, :, ln].astype(F32)
            pad_ref[t, :, 8 + cols : 11 + cols] = right_ref[:, :, ln].astype(F32)

    @pl.when(odd_ref[1] == 0)
    def _():
        place(far_cols_ref, near_cols_ref)

    @pl.when(odd_ref[1] != 0)
    def _():
        place(near_cols_ref, far_cols_ref)


def convolve(pad_ref, k_ref, out_ref, rows, cols, flip):
    blocks = 4
    for t in range(2):
        ln = slice(t * LANES, (t + 1) * LANES)

        def step(n, carry, t=t, ln=ln):
            at = pl.multiple_of(n * 8 * blocks, 8)
            acc = [[jnp.zeros((8, LANES), F32) for _ in range(rows)] for _ in range(blocks)]
            for j in range(7):
                window = [
                    [pad_ref[t, r, pl.ds(at + 8 * b + 5 + j, 8), :] for r in range(rows + 6)] for b in range(blocks)
                ]
                for i in range(7):
                    row, col = (6 - i, 6 - j) if flip else (i, j)
                    weight = k_ref[row, col : col + 1, ln]
                    for b in range(blocks):
                        for p in range(rows):
                            acc[b][p] = acc[b][p] + window[b][p + i] * weight
            for b in range(blocks):
                for p in range(rows):
                    out_ref[t, p, pl.ds(at + 8 * b, 8), :] = acc[b][p]
            return carry

        lax.fori_loop(0, cols // (8 * blocks), step, 0)


def kernel_sums(pad_ref, grad_ref, small_ref, rows, cols):
    for t in range(2):
        for j in range(7):
            acc = [jnp.zeros((8, LANES), F32) for _ in range(7)]
            for b in range(cols // 8):
                window = [pad_ref[t, r, b * 8 + 5 + j : b * 8 + 13 + j, :] for r in range(rows + 6)]
                grad = [grad_ref[t, p, b * 8 : b * 8 + 8, :] for p in range(rows)]
                for i in range(7):
                    part = window[i] * grad[0]
                    for p in range(1, rows):
                        part = part + window[p + i] * grad[p]
                    acc[i] = acc[i] + part
            for i in range(7):
                at = t * 64 + j * 7 + i
                small_ref[at : at + 1, :] = jnp.sum(acc[i], axis=0, keepdims=True)


def write_chunks(chunk_ref, base, part):
    for n in range(part.shape[0] // BIG_ROWS):
        chunk_ref[base + n] = part[n * BIG_ROWS : (n + 1) * BIG_ROWS]


def block_kernel(
    odd_ref, own_ref, near_rows_ref, far_rows_ref, near_cols_ref, far_cols_ref, mask_ref, masked_ref, k_ref, dw_bias_ref,
    gain_ref, bias_ref, w_in_ref, b_in_ref, w_out_hbm_ref, b_out_ref, scale_ref,
    out_ref, grad_ref, chunk_ref, singles_ref,
    pad_ref, depth_ref, w_out_ref, w_out_sem,
):
    rows, cols, channels = own_ref.shape
    cells = rows * cols
    hidden = w_in_ref.shape[1]
    halves = channels // LANES
    w_out_copy = pltpu.make_async_copy(w_out_hbm_ref, w_out_ref, w_out_sem)
    w_out_copy.start()
    fill_padded(odd_ref, pad_ref, own_ref, near_rows_ref, far_rows_ref, near_cols_ref, far_cols_ref)
    convolve(pad_ref, k_ref, depth_ref, rows, cols, False)
    depth = jnp.concatenate([depth_ref[t].reshape(cells, LANES) for t in range(2)], axis=1)
    depth = depth + dw_bias_ref[...]
    center = depth - jnp.mean(depth, axis=-1, keepdims=True)
    inv_std = lax.rsqrt(jnp.mean(center * center, axis=-1, keepdims=True) + 1e-6)
    norm_hat = center * inv_std
    normed = (norm_hat * gain_ref[...] + bias_ref[...]).astype(BF16)
    masked = masked_ref[...].astype(F32)
    grad_branch = (masked * scale_ref[...]).astype(BF16)
    branch = jnp.zeros((cells, channels), F32)
    grad_norm = jnp.zeros((cells, channels), F32)
    root = math.sqrt(2.0 / math.pi)
    w_out_copy.wait()
    b_in_sums = []
    width = channels
    for h in range(hidden // width):
        at = slice(h * width, (h + 1) * width)
        w_in = w_in_ref[:, at]
        w_out = w_out_ref[at, :]
        pre = dot(normed, w_in, 1, 0) + b_in_ref[:, at]
        square = pre * pre
        bent = jnp.tanh(root * pre * (1.0 + 0.044715 * square))
        half = 0.5 * (1.0 + bent)
        act = (pre * half).astype(BF16)
        slope = half + (0.5 * root) * pre * (1.0 - bent * bent) * (1.0 + (3 * 0.044715) * square)
        grad_pre = (dot(grad_branch, w_out, 1, 1) * slope).astype(BF16)
        branch = branch + dot(act, w_out, 1, 0)
        grad_norm = grad_norm + dot(grad_pre, w_in, 1, 1)
        g_in = dot(normed, grad_pre, 0, 0).astype(BF16)
        g_out = dot(act, grad_branch, 0, 0).astype(BF16)
        for t in range(width // LANES):
            base = (h * (width // LANES) + t) * (channels // BIG_ROWS)
            write_chunks(chunk_ref, base, g_in[:, t * LANES : (t + 1) * LANES])
        for t in range(halves):
            base = (hidden * halves + t * hidden + h * width) // BIG_ROWS
            write_chunks(chunk_ref, base, g_out[:, t * LANES : (t + 1) * LANES])
        b_in_sums.append(jnp.sum(grad_pre.astype(F32), axis=0, keepdims=True))
    branch = branch + b_out_ref[...]
    mask = mask_ref[...].astype(F32)
    own = own_ref[...].reshape(cells, channels).astype(F32)
    out_ref[...] = (own + mask * scale_ref[...] * branch).astype(BF16).reshape(rows, cols, channels)
    scaled = grad_norm * gain_ref[...]
    mean_u = jnp.mean(scaled, axis=-1, keepdims=True)
    mean_un = jnp.mean(scaled * norm_hat, axis=-1, keepdims=True)
    grad_depth = (inv_std * (scaled - mean_u - norm_hat * mean_un)).astype(BF16)
    grad_ref[...] = grad_depth.reshape(rows, cols, channels)
    grad_float = grad_depth.astype(F32)
    singles = b_in_sums + [
        jnp.sum(grad_float, axis=0, keepdims=True),
        jnp.sum(grad_norm * norm_hat, axis=0, keepdims=True),
        jnp.sum(grad_norm, axis=0, keepdims=True),
        jnp.sum(grad_branch.astype(F32), axis=0, keepdims=True),
        jnp.sum(masked * branch, axis=0, keepdims=True),
    ]
    for n, single in enumerate(singles):
        singles_ref[n : n + 1, :] = single


def sums_kernel(
    odd_ref, own_ref, near_rows_ref, far_rows_ref, near_cols_ref, far_cols_ref, grad_ref, singles_ref, out_ref,
    pad_ref, grad_float_ref, small_ref,
):
    rows, cols, _ = own_ref.shape
    singles = singles_ref.shape[0]
    fill_padded(odd_ref, pad_ref, own_ref, near_rows_ref, far_rows_ref, near_cols_ref, far_cols_ref)
    for t in range(2):
        ln = slice(t * LANES, (t + 1) * LANES)
        grad_float_ref[t] = grad_ref[:, :, ln].astype(F32)
        small_ref[t * 64 + 49 : t * 64 + 49 + singles, :] = singles_ref[:, ln]
        small_ref[t * 64 + 49 + singles : t * 64 + 64, :] = jnp.zeros((15 - singles, LANES), F32)
    kernel_sums(pad_ref, grad_float_ref, small_ref, rows, cols)
    out_ref[0:16] = small_ref[...].reshape(16, 8, LANES).astype(BF16)
    out_ref[16:] = jnp.zeros((out_ref.shape[0] - 16, 8, LANES), BF16)


def merge_kernel(pair_ref, small_ref, out_ref):
    out_ref[:, 0:BIG_ROWS, :] = (pair_ref[0].astype(F32) + pair_ref[1].astype(F32)).astype(BF16)
    out_ref[:, BIG_ROWS:, :] = small_ref[...]


def state_kernel(
    odd_ref, own_ref, near_rows_ref, far_rows_ref, near_cols_ref, far_cols_ref, cot_ref, k_ref, out_ref, pad_ref, sum_ref
):
    rows, cols, _ = own_ref.shape
    fill_padded(odd_ref, pad_ref, own_ref, near_rows_ref, far_rows_ref, near_cols_ref, far_cols_ref)
    convolve(pad_ref, k_ref, sum_ref, rows, cols, True)
    for t in range(2):
        ln = slice(t * LANES, (t + 1) * LANES)
        out_ref[:, :, ln] = (cot_ref[:, :, ln].astype(F32) + sum_ref[t]).astype(BF16)


def unpack_kernel(
    factor, core_ref, mine_ref, other_ref, k_ref, one_ref, two_ref, three_ref, w_in_ref, b_in_ref, w_out_ref, four_ref,
    five_ref, small_ref,
):
    channels, hidden = w_in_ref.shape

    def rows_of(ref, at, size):
        part = ref[at // BIG_ROWS : (at + size) // BIG_ROWS, 0:BIG_ROWS, :]
        return part.astype(F32).reshape(size, LANES) * factor

    def write(first_ref, second_ref):
        for t in range(hidden // LANES):
            w_in_ref[:, t * LANES : (t + 1) * LANES] = rows_of(first_ref, t * channels, channels)
        for t in range(channels // LANES):
            w_out_ref[:, t * LANES : (t + 1) * LANES] = rows_of(second_ref, t * hidden, hidden)

    @pl.when(core_ref[0] == 0)
    def _():
        write(mine_ref, other_ref)

    @pl.when(core_ref[0] != 0)
    def _():
        write(other_ref, mine_ref)

    small = mine_ref[0:16, BIG_ROWS:, :].astype(F32) + other_ref[0:16, BIG_ROWS:, :].astype(F32)
    small_ref[...] = small.reshape(128, LANES) * factor
    blocks = hidden // channels
    for t in range(2):
        ln = slice(t * LANES, (t + 1) * LANES)
        for j in range(7):
            for i in range(7):
                at = t * 64 + j * 7 + i
                k_ref[i, j : j + 1, ln] = small_ref[at : at + 1, :]
        at = t * 64 + 49
        for n in range(blocks):
            part = slice(n * channels + t * LANES, n * channels + (t + 1) * LANES)
            b_in_ref[:, part] = small_ref[at + n : at + n + 1, :]
        for n, ref in enumerate((one_ref, two_ref, three_ref, four_ref, five_ref)):
            ref[:, ln] = small_ref[at + blocks + n : at + blocks + n + 1, :]


def groups_along(first_core, second_core):
    index = np.arange(math.prod(SIZES.values())).reshape(tuple(SIZES.values()))
    groups = []
    for core, axes in enumerate((first_core, second_core)):
        mine = index.take(core, axis=EVERY.index("core"))
        names = [name for name in EVERY if name != "core"]
        order = [name for name in names if name not in axes] + list(axes)
        size = math.prod(SIZES[name] for name in axes)
        groups += mine.transpose([names.index(name) for name in order]).reshape(-1, size).tolist()
    return groups


PLANE = groups_along(("x", "z"), ("x", "y_hi", "y_lo"))
COLUMN = groups_along(("y_hi", "y_lo"), ("z",))


def exchange(value, groups):
    return lax.all_to_all(value, EVERY, 0, 0, axis_index_groups=groups)


def swaps(axis, wrap):
    size = lax.axis_size(axis)
    near = [(i, i ^ 1) for i in range(size)]
    far = []
    for i in range(1, size if wrap else size - 1, 2):
        far += [(i, (i + 1) % size), ((i + 1) % size, i)]
    return near, far


def swap_rows(field, odd):
    rows = field.shape[0]
    near, far = swaps(LAT, False)
    first, last = field[:3], field[rows - 3 :]
    far_rows = lax.ppermute(jnp.where(odd, last, first), LAT, far)
    near_rows = lax.ppermute(jnp.where(odd, first, last), LAT, near)
    return near_rows, far_rows


def swap_cols(field, near_rows, far_rows, odd_lat, odd_lon):
    cols = field.shape[1]
    near, far = swaps(LON, True)

    def strip(at):
        part = slice(at, at + 3)
        before = jnp.where(odd_lat, near_rows[:, part], far_rows[:, part])
        after = jnp.where(odd_lat, far_rows[:, part], near_rows[:, part])
        return jnp.concatenate([before, field[:, part], after], axis=0)

    first, last = strip(0), strip(cols - 3)
    far_cols = lax.ppermute(jnp.where(odd_lon, last, first), LON, far)
    near_cols = lax.ppermute(jnp.where(odd_lon, first, last), LON, near)
    return near_cols, far_cols


def local(
    ocean_state, land_sea, cotangent, dw_kernel, dw_bias, ln_gain, ln_bias, w_in, b_in, w_out, b_out, layer_scale
):
    _, rows, cols, channels = ocean_state.shape
    cells = rows * cols
    hidden = w_in.shape[1]
    plane, column = len(PLANE[0]), len(COLUMN[0])
    core = lax.axis_index("core")
    own = ocean_state[0]
    cot = cotangent[0]
    odd_lat = lax.axis_index("z") & 1
    odd = jnp.stack([odd_lat, core]).astype(jnp.int32)
    odd_lat, odd_lon = odd_lat == 1, core == 1
    near_rows, far_rows = swap_rows(own, odd_lat)
    near_cols, far_cols = swap_cols(own, near_rows, far_rows, odd_lat, odd_lon)
    mask = jnp.broadcast_to(land_sea[0].astype(BF16)[..., None], cot.shape)
    masked = mask * cot
    pad = pltpu.VMEM((2, rows + 6, cols + 16, LANES), F32)
    cells_scratch = pltpu.VMEM((2, rows, cols, LANES), F32)
    smem, vmem = pl.BlockSpec(memory_space=pltpu.SMEM), pl.BlockSpec(memory_space=pltpu.VMEM)
    params = pltpu.CompilerParams(vmem_limit_bytes=VMEM_BYTES)
    blocks = hidden // channels
    output, grad_depth, chunks, singles = pl.pallas_call(
        block_kernel,
        out_shape=(
            jax.ShapeDtypeStruct((rows, cols, channels), BF16),
            jax.ShapeDtypeStruct((rows, cols, channels), BF16),
            jax.ShapeDtypeStruct((2 * plane, BIG_ROWS, LANES), BF16),
            jax.ShapeDtypeStruct((blocks + 5, channels), F32),
        ),
        in_specs=[smem] + [vmem] * 13 + [pl.BlockSpec(memory_space=pltpu.HBM)] + [vmem] * 2,
        scratch_shapes=[
            pad,
            cells_scratch,
            pltpu.VMEM(w_out.shape, BF16),
            pltpu.SemaphoreType.DMA,
        ],
        compiler_params=params,
        cost_estimate=pl.CostEstimate(flops=1300000000, transcendentals=400000, bytes_accessed=6000000),
        name="block",
    )(
        odd, own, near_rows, far_rows, near_cols, far_cols, mask.reshape(cells, channels), masked.reshape(cells, channels), dw_kernel,
        dw_bias[None], ln_gain[None], ln_bias[None], w_in, b_in[None], pltpu.with_memory_space_constraint(w_out, pltpu.HBM), b_out[None], layer_scale[None],
    )
    rows_sent = swap_rows(grad_depth, odd_lat)
    small = pl.pallas_call(
        sums_kernel,
        out_shape=jax.ShapeDtypeStruct((plane, CHUNK_ROWS - BIG_ROWS, LANES), BF16),
        in_specs=[smem] + [vmem] * 7,
        scratch_shapes=[pad, cells_scratch, pltpu.VMEM((128, LANES), F32)],
        compiler_params=params,
        cost_estimate=pl.CostEstimate(flops=10000000, transcendentals=0, bytes_accessed=3000000),
        name="sums",
    )(odd, own, near_rows, far_rows, near_cols, far_cols, grad_depth, singles)
    pair = lax.all_to_all(chunks.reshape(2, plane, BIG_ROWS, LANES), "core", 0, 0)
    pair, small = lax.optimization_barrier((pair, small))
    value = pl.pallas_call(
        merge_kernel,
        out_shape=jax.ShapeDtypeStruct((plane, CHUNK_ROWS, LANES), BF16),
        compiler_params=params,
        cost_estimate=pl.CostEstimate(flops=300000, transcendentals=0, bytes_accessed=2000000),
        name="merge",
    )(pair, small)
    value = exchange(value, PLANE)
    value = jnp.sum(value.astype(F32), axis=0).astype(BF16)
    value, rows_sent = lax.optimization_barrier((value, rows_sent))
    value = exchange(jnp.broadcast_to(value[None], (column,) + value.shape), COLUMN)
    value = jnp.sum(value.astype(F32), axis=0).astype(BF16)
    value = exchange(jnp.broadcast_to(value[None], (plane,) + value.shape), PLANE)
    cols_sent = swap_cols(grad_depth, *rows_sent, odd_lat, odd_lon)
    grad_state = pl.pallas_call(
        state_kernel,
        out_shape=jax.ShapeDtypeStruct((rows, cols, channels), BF16),
        in_specs=[smem] + [vmem] * 7,
        scratch_shapes=[pad, cells_scratch],
        compiler_params=params,
        cost_estimate=pl.CostEstimate(flops=10000000, transcendentals=0, bytes_accessed=3000000),
        name="state",
    )(odd, grad_depth, *rows_sent, *cols_sent, cot, dw_kernel)
    value, grad_state = lax.optimization_barrier((value, grad_state))
    other = lax.ppermute(value, "core", [(0, 1), (1, 0)])
    total_cells = cells * lax.axis_size(LON) * lax.axis_size(LAT)
    factor = 1.0 / math.sqrt(total_cells)
    single = jax.ShapeDtypeStruct((1, channels), F32)
    sums = pl.pallas_call(
        functools.partial(unpack_kernel, factor),
        out_shape=(
            jax.ShapeDtypeStruct(dw_kernel.shape, F32),
            single,
            single,
            single,
            jax.ShapeDtypeStruct((channels, hidden), F32),
            jax.ShapeDtypeStruct((1, hidden), F32),
            jax.ShapeDtypeStruct((hidden, channels), F32),
            single,
            single,
        ),
        in_specs=[smem, vmem, vmem],
        scratch_shapes=[pltpu.VMEM((128, LANES), F32)],
        compiler_params=params,
        name="unpack",
    )(core.astype(jnp.int32).reshape(1), value, other)
    sums = [part[0] if part.shape[0] == 1 else part for part in sums]
    return (output[None], grad_state[None], *sums)


def solution(mesh):
    mesh = Mesh(mesh.devices.reshape(tuple(SIZES.values())), EVERY)
    field = P(None, LAT, LON, None)
    in_specs = (field, P(None, LAT, LON), field) + (P(),) * 9
    out_specs = (field, field) + (P(),) * 9
    return jax.shard_map(local, mesh=mesh, in_specs=in_specs, out_specs=out_specs, check_vma=False)
```

```python
import functools
import math

import jax
import jax.numpy as jnp
import numpy as np
from jax import lax
from jax.experimental import pallas as pl
from jax.experimental.pallas import tpu as pltpu
from jax.sharding import Mesh, PartitionSpec as P

LON = ("y_lo", "core")
LAT = ("x", "y_hi", "z")
SIZES = {"y_lo": 4, "core": 2, "x": 4, "y_hi": 2, "z": 8}
EVERY = tuple(SIZES)
BIG_ROWS = 64
CHUNK_ROWS = 72
LANES = 128
VMEM_BYTES = 32 << 20
F32 = jnp.float32
BF16 = jnp.bfloat16


def dot(a, b, ca, cb):
    return lax.dot_general(a, b, (((ca,), (cb,)), ((), ())), preferred_element_type=F32)


def fill_rows(odd_ref, pad_ref, own_ref, near_rows_ref, far_rows_ref, parts):
    rows = own_ref.shape[0]
    low = rows + 3
    near_at = jnp.where(odd_ref[0] == 1, 0, low)
    far_at = low - near_at
    for t in range(2):
        ln = slice(t * LANES, (t + 1) * LANES)
        for at, end in parts:
            pad_ref[t, 3 : 3 + rows, 8 + at : 8 + end] = own_ref[:, at:end, ln].astype(F32)
            pad_ref[t, pl.ds(near_at, 3), 8 + at : 8 + end] = near_rows_ref[:, at:end, ln].astype(F32)
            pad_ref[t, pl.ds(far_at, 3), 8 + at : 8 + end] = far_rows_ref[:, at:end, ln].astype(F32)


def fill_cols(odd_ref, pad_ref, cols, near_cols_ref, far_cols_ref):
    def place(left_ref, right_ref):
        for t in range(2):
            ln = slice(t * LANES, (t + 1) * LANES)
            pad_ref[t, :, 5:8] = left_ref[:, :, ln].astype(F32)
            pad_ref[t, :, 8 + cols : 11 + cols] = right_ref[:, :, ln].astype(F32)

    @pl.when(odd_ref[1] == 0)
    def _():
        place(far_cols_ref, near_cols_ref)

    @pl.when(odd_ref[1] != 0)
    def _():
        place(near_cols_ref, far_cols_ref)


def fill_padded(odd_ref, pad_ref, own_ref, near_rows_ref, far_rows_ref, near_cols_ref, far_cols_ref):
    cols = own_ref.shape[1]
    fill_rows(odd_ref, pad_ref, own_ref, near_rows_ref, far_rows_ref, ((0, cols),))
    fill_cols(odd_ref, pad_ref, cols, near_cols_ref, far_cols_ref)


def convolve(pad_ref, k_ref, out_ref, rows, first, steps, offsets, flip):
    stride = offsets[-1] + 8
    for t in range(2):
        ln = slice(t * LANES, (t + 1) * LANES)

        def step(n, carry, t=t, ln=ln):
            at = pl.multiple_of(n * stride, 8)
            acc = [[jnp.zeros((8, LANES), F32) for _ in range(rows)] for _ in offsets]
            for j in range(7):
                window = [
                    [pad_ref[t, r, pl.ds(at + first + off + 5 + j, 8), :] for r in range(rows + 6)] for off in offsets
                ]
                for i in range(7):
                    row, col = (6 - i, 6 - j) if flip else (i, j)
                    weight = k_ref[row, col : col + 1, ln]
                    for b in range(len(offsets)):
                        for p in range(rows):
                            acc[b][p] = acc[b][p] + window[b][p + i] * weight
            for b, off in enumerate(offsets):
                for p in range(rows):
                    out_ref[t, p, pl.ds(at + off, 8), :] = acc[b][p]
            return carry

        lax.fori_loop(0, steps, step, 0)


def inner_kernel(odd_ref, own_ref, near_rows_ref, far_rows_ref, k_ref, out_ref, pad_ref):
    rows, cols, _ = own_ref.shape
    fill_rows(odd_ref, pad_ref, own_ref, near_rows_ref, far_rows_ref, ((0, cols),))
    convolve(pad_ref, k_ref, out_ref, rows, 8, 2, (0, 8, 16), False)


def kernel_sums(pad_ref, grad_ref, small_ref, rows, cols):
    for t in range(2):
        for j in range(7):
            acc = [jnp.zeros((8, LANES), F32) for _ in range(7)]
            for b in range(cols // 8):
                window = [pad_ref[t, r, b * 8 + 5 + j : b * 8 + 13 + j, :] for r in range(rows + 6)]
                grad = [grad_ref[t, p, b * 8 : b * 8 + 8, :] for p in range(rows)]
                for i in range(7):
                    part = window[i] * grad[0]
                    for p in range(1, rows):
                        part = part + window[p + i] * grad[p]
                    acc[i] = acc[i] + part
            for i in range(7):
                at = t * 64 + j * 7 + i
                small_ref[at : at + 1, :] = jnp.sum(acc[i], axis=0, keepdims=True)


def write_chunks(chunk_ref, base, part):
    for n in range(part.shape[0] // BIG_ROWS):
        chunk_ref[base + n] = part[n * BIG_ROWS : (n + 1) * BIG_ROWS]


def block_kernel(
    odd_ref, own_ref, near_rows_ref, far_rows_ref, near_cols_ref, far_cols_ref, inner_ref, mask_ref, masked_ref, k_ref, dw_bias_ref,
    gain_ref, bias_ref, w_in_ref, b_in_ref, w_out_hbm_ref, b_out_ref, scale_ref,
    out_ref, grad_ref, chunk_ref, singles_ref,
    pad_ref, depth_ref, w_out_ref, w_out_sem,
):
    rows, cols, channels = own_ref.shape
    cells = rows * cols
    hidden = w_in_ref.shape[1]
    halves = channels // LANES
    w_out_copy = pltpu.make_async_copy(w_out_hbm_ref, w_out_ref, w_out_sem)
    w_out_copy.start()
    fill_rows(odd_ref, pad_ref, own_ref, near_rows_ref, far_rows_ref, ((0, 16), (cols - 16, cols)))
    fill_cols(odd_ref, pad_ref, cols, near_cols_ref, far_cols_ref)
    convolve(pad_ref, k_ref, depth_ref, rows, 0, 1, (0, cols - 8), False)
    depth_ref[:, :, 8 : cols - 8] = inner_ref[...]
    depth = jnp.concatenate([depth_ref[t].reshape(cells, LANES) for t in range(2)], axis=1)
    depth = depth + dw_bias_ref[...]
    center = depth - jnp.mean(depth, axis=-1, keepdims=True)
    inv_std = lax.rsqrt(jnp.mean(center * center, axis=-1, keepdims=True) + 1e-6)
    norm_hat = center * inv_std
    normed = (norm_hat * gain_ref[...] + bias_ref[...]).astype(BF16)
    masked = masked_ref[...].astype(F32)
    grad_branch = (masked * scale_ref[...]).astype(BF16)
    branch = jnp.zeros((cells, channels), F32)
    grad_norm = jnp.zeros((cells, channels), F32)
    root = math.sqrt(2.0 / math.pi)
    w_out_copy.wait()
    b_in_sums = []
    width = channels
    for h in range(hidden // width):
        at = slice(h * width, (h + 1) * width)
        w_in = w_in_ref[:, at]
        w_out = w_out_ref[at, :]
        pre = dot(normed, w_in, 1, 0) + b_in_ref[:, at]
        square = pre * pre
        bent = jnp.tanh(root * pre * (1.0 + 0.044715 * square))
        half = 0.5 * (1.0 + bent)
        act = (pre * half).astype(BF16)
        slope = half + (0.5 * root) * pre * (1.0 - bent * bent) * (1.0 + (3 * 0.044715) * square)
        grad_pre = (dot(grad_branch, w_out, 1, 1) * slope).astype(BF16)
        branch = branch + dot(act, w_out, 1, 0)
        grad_norm = grad_norm + dot(grad_pre, w_in, 1, 1)
        g_in = dot(normed, grad_pre, 0, 0).astype(BF16)
        g_out = dot(act, grad_branch, 0, 0).astype(BF16)
        for t in range(width // LANES):
            base = (h * (width // LANES) + t) * (channels // BIG_ROWS)
            write_chunks(chunk_ref, base, g_in[:, t * LANES : (t + 1) * LANES])
        for t in range(halves):
            base = (hidden * halves + t * hidden + h * width) // BIG_ROWS
            write_chunks(chunk_ref, base, g_out[:, t * LANES : (t + 1) * LANES])
        b_in_sums.append(jnp.sum(grad_pre.astype(F32), axis=0, keepdims=True))
    branch = branch + b_out_ref[...]
    mask = mask_ref[...].astype(F32)
    own = own_ref[...].reshape(cells, channels).astype(F32)
    out_ref[...] = (own + mask * scale_ref[...] * branch).astype(BF16).reshape(rows, cols, channels)
    scaled = grad_norm * gain_ref[...]
    mean_u = jnp.mean(scaled, axis=-1, keepdims=True)
    mean_un = jnp.mean(scaled * norm_hat, axis=-1, keepdims=True)
    grad_depth = (inv_std * (scaled - mean_u - norm_hat * mean_un)).astype(BF16)
    grad_ref[...] = grad_depth.reshape(rows, cols, channels)
    grad_float = grad_depth.astype(F32)
    singles = b_in_sums + [
        jnp.sum(grad_float, axis=0, keepdims=True),
        jnp.sum(grad_norm * norm_hat, axis=0, keepdims=True),
        jnp.sum(grad_norm, axis=0, keepdims=True),
        jnp.sum(grad_branch.astype(F32), axis=0, keepdims=True),
        jnp.sum(masked * branch, axis=0, keepdims=True),
    ]
    for n, single in enumerate(singles):
        singles_ref[n : n + 1, :] = single


def sums_kernel(
    odd_ref, own_ref, near_rows_ref, far_rows_ref, near_cols_ref, far_cols_ref, grad_ref, singles_ref, out_ref,
    pad_ref, grad_float_ref, small_ref,
):
    rows, cols, _ = own_ref.shape
    singles = singles_ref.shape[0]
    fill_padded(odd_ref, pad_ref, own_ref, near_rows_ref, far_rows_ref, near_cols_ref, far_cols_ref)
    for t in range(2):
        ln = slice(t * LANES, (t + 1) * LANES)
        grad_float_ref[t] = grad_ref[:, :, ln].astype(F32)
        small_ref[t * 64 + 49 : t * 64 + 49 + singles, :] = singles_ref[:, ln]
        small_ref[t * 64 + 49 + singles : t * 64 + 64, :] = jnp.zeros((15 - singles, LANES), F32)
    kernel_sums(pad_ref, grad_float_ref, small_ref, rows, cols)
    out_ref[0:16] = small_ref[...].reshape(16, 8, LANES).astype(BF16)
    out_ref[16:] = jnp.zeros((out_ref.shape[0] - 16, 8, LANES), BF16)


def merge_kernel(pair_ref, small_ref, out_ref):
    out_ref[:, 0:BIG_ROWS, :] = (pair_ref[0].astype(F32) + pair_ref[1].astype(F32)).astype(BF16)
    out_ref[:, BIG_ROWS:, :] = small_ref[...]


def state_kernel(
    odd_ref, own_ref, near_rows_ref, far_rows_ref, near_cols_ref, far_cols_ref, cot_ref, k_ref, out_ref, pad_ref, sum_ref
):
    rows, cols, _ = own_ref.shape
    fill_padded(odd_ref, pad_ref, own_ref, near_rows_ref, far_rows_ref, near_cols_ref, far_cols_ref)
    convolve(pad_ref, k_ref, sum_ref, rows, 0, 2, (0, 8, 16, 24), True)
    for t in range(2):
        ln = slice(t * LANES, (t + 1) * LANES)
        out_ref[:, :, ln] = (cot_ref[:, :, ln].astype(F32) + sum_ref[t]).astype(BF16)


def unpack_kernel(
    factor, core_ref, mine_ref, other_ref, k_ref, one_ref, two_ref, three_ref, w_in_ref, b_in_ref, w_out_ref, four_ref,
    five_ref, small_ref,
):
    channels, hidden = w_in_ref.shape

    def rows_of(ref, at, size):
        part = ref[at // BIG_ROWS : (at + size) // BIG_ROWS, 0:BIG_ROWS, :]
        return part.astype(F32).reshape(size, LANES) * factor

    def write(first_ref, second_ref):
        for t in range(hidden // LANES):
            w_in_ref[:, t * LANES : (t + 1) * LANES] = rows_of(first_ref, t * channels, channels)
        for t in range(channels // LANES):
            w_out_ref[:, t * LANES : (t + 1) * LANES] = rows_of(second_ref, t * hidden, hidden)

    @pl.when(core_ref[0] == 0)
    def _():
        write(mine_ref, other_ref)

    @pl.when(core_ref[0] != 0)
    def _():
        write(other_ref, mine_ref)

    small = mine_ref[0:16, BIG_ROWS:, :].astype(F32) + other_ref[0:16, BIG_ROWS:, :].astype(F32)
    small_ref[...] = small.reshape(128, LANES) * factor
    blocks = hidden // channels
    for t in range(2):
        ln = slice(t * LANES, (t + 1) * LANES)
        for j in range(7):
            for i in range(7):
                at = t * 64 + j * 7 + i
                k_ref[i, j : j + 1, ln] = small_ref[at : at + 1, :]
        at = t * 64 + 49
        for n in range(blocks):
            part = slice(n * channels + t * LANES, n * channels + (t + 1) * LANES)
            b_in_ref[:, part] = small_ref[at + n : at + n + 1, :]
        for n, ref in enumerate((one_ref, two_ref, three_ref, four_ref, five_ref)):
            ref[:, ln] = small_ref[at + blocks + n : at + blocks + n + 1, :]


def groups_along(first_core, second_core):
    index = np.arange(math.prod(SIZES.values())).reshape(tuple(SIZES.values()))
    groups = []
    for core, axes in enumerate((first_core, second_core)):
        mine = index.take(core, axis=EVERY.index("core"))
        names = [name for name in EVERY if name != "core"]
        order = [name for name in names if name not in axes] + list(axes)
        size = math.prod(SIZES[name] for name in axes)
        groups += mine.transpose([names.index(name) for name in order]).reshape(-1, size).tolist()
    return groups


PLANE = groups_along(("x", "z"), ("x", "y_hi", "y_lo"))
COLUMN = groups_along(("y_hi", "y_lo"), ("z",))


def exchange(value, groups):
    return lax.all_to_all(value, EVERY, 0, 0, axis_index_groups=groups)


def swaps(axis, wrap):
    size = lax.axis_size(axis)
    near = [(i, i ^ 1) for i in range(size)]
    far = []
    for i in range(1, size if wrap else size - 1, 2):
        far += [(i, (i + 1) % size), ((i + 1) % size, i)]
    return near, far


def swap_rows(field, odd):
    rows = field.shape[0]
    near, far = swaps(LAT, False)
    first, last = field[:3], field[rows - 3 :]
    far_rows = lax.ppermute(jnp.where(odd, last, first), LAT, far)
    near_rows = lax.ppermute(jnp.where(odd, first, last), LAT, near)
    return near_rows, far_rows


def swap_cols(field, near_rows, far_rows, odd_lat, odd_lon):
    cols = field.shape[1]
    near, far = swaps(LON, True)

    def strip(at):
        part = slice(at, at + 3)
        before = jnp.where(odd_lat, near_rows[:, part], far_rows[:, part])
        after = jnp.where(odd_lat, far_rows[:, part], near_rows[:, part])
        return jnp.concatenate([before, field[:, part], after], axis=0)

    first, last = strip(0), strip(cols - 3)
    far_cols = lax.ppermute(jnp.where(odd_lon, last, first), LON, far)
    near_cols = lax.ppermute(jnp.where(odd_lon, first, last), LON, near)
    return near_cols, far_cols


def local(
    ocean_state, land_sea, cotangent, dw_kernel, dw_bias, ln_gain, ln_bias, w_in, b_in, w_out, b_out, layer_scale
):
    _, rows, cols, channels = ocean_state.shape
    cells = rows * cols
    hidden = w_in.shape[1]
    plane, column = len(PLANE[0]), len(COLUMN[0])
    core = lax.axis_index("core")
    own = ocean_state[0]
    cot = cotangent[0]
    odd_lat = lax.axis_index("z") & 1
    odd = jnp.stack([odd_lat, core]).astype(jnp.int32)
    odd_lat, odd_lon = odd_lat == 1, core == 1
    near_rows, far_rows = swap_rows(own, odd_lat)
    near_cols, far_cols = swap_cols(own, near_rows, far_rows, odd_lat, odd_lon)
    mask = jnp.broadcast_to(land_sea[0].astype(BF16)[..., None], cot.shape)
    masked = mask * cot
    pad = pltpu.VMEM((2, rows + 6, cols + 16, LANES), F32)
    cells_scratch = pltpu.VMEM((2, rows, cols, LANES), F32)
    smem, vmem = pl.BlockSpec(memory_space=pltpu.SMEM), pl.BlockSpec(memory_space=pltpu.VMEM)
    params = pltpu.CompilerParams(vmem_limit_bytes=VMEM_BYTES)
    inner = pl.pallas_call(
        inner_kernel,
        out_shape=jax.ShapeDtypeStruct((2, rows, cols - 16, LANES), F32),
        in_specs=[smem] + [vmem] * 4,
        scratch_shapes=[pad],
        compiler_params=params,
        cost_estimate=pl.CostEstimate(flops=10000000, transcendentals=0, bytes_accessed=2000000),
        name="inner",
    )(odd, own, near_rows, far_rows, dw_kernel)
    blocks = hidden // channels
    output, grad_depth, chunks, singles = pl.pallas_call(
        block_kernel,
        out_shape=(
            jax.ShapeDtypeStruct((rows, cols, channels), BF16),
            jax.ShapeDtypeStruct((rows, cols, channels), BF16),
            jax.ShapeDtypeStruct((2 * plane, BIG_ROWS, LANES), BF16),
            jax.ShapeDtypeStruct((blocks + 5, channels), F32),
        ),
        in_specs=[smem] + [vmem] * 14 + [pl.BlockSpec(memory_space=pltpu.HBM)] + [vmem] * 2,
        scratch_shapes=[
            pad,
            cells_scratch,
            pltpu.VMEM(w_out.shape, BF16),
            pltpu.SemaphoreType.DMA,
        ],
        compiler_params=params,
        cost_estimate=pl.CostEstimate(flops=1300000000, transcendentals=400000, bytes_accessed=6000000),
        name="block",
    )(
        odd, own, near_rows, far_rows, near_cols, far_cols, inner, mask.reshape(cells, channels), masked.reshape(cells, channels), dw_kernel,
        dw_bias[None], ln_gain[None], ln_bias[None], w_in, b_in[None], pltpu.with_memory_space_constraint(w_out, pltpu.HBM), b_out[None], layer_scale[None],
    )
    rows_sent = swap_rows(grad_depth, odd_lat)
    small = pl.pallas_call(
        sums_kernel,
        out_shape=jax.ShapeDtypeStruct((plane, CHUNK_ROWS - BIG_ROWS, LANES), BF16),
        in_specs=[smem] + [vmem] * 7,
        scratch_shapes=[pad, cells_scratch, pltpu.VMEM((128, LANES), F32)],
        compiler_params=params,
        cost_estimate=pl.CostEstimate(flops=10000000, transcendentals=0, bytes_accessed=3000000),
        name="sums",
    )(odd, own, near_rows, far_rows, near_cols, far_cols, grad_depth, singles)
    pair = lax.all_to_all(chunks.reshape(2, plane, BIG_ROWS, LANES), "core", 0, 0)
    pair, small = lax.optimization_barrier((pair, small))
    value = pl.pallas_call(
        merge_kernel,
        out_shape=jax.ShapeDtypeStruct((plane, CHUNK_ROWS, LANES), BF16),
        compiler_params=params,
        cost_estimate=pl.CostEstimate(flops=300000, transcendentals=0, bytes_accessed=2000000),
        name="merge",
    )(pair, small)
    value = exchange(value, PLANE)
    value = jnp.sum(value.astype(F32), axis=0).astype(BF16)
    value, rows_sent = lax.optimization_barrier((value, rows_sent))
    value = exchange(jnp.broadcast_to(value[None], (column,) + value.shape), COLUMN)
    value = jnp.sum(value.astype(F32), axis=0).astype(BF16)
    value = exchange(jnp.broadcast_to(value[None], (plane,) + value.shape), PLANE)
    cols_sent = swap_cols(grad_depth, *rows_sent, odd_lat, odd_lon)
    grad_state = pl.pallas_call(
        state_kernel,
        out_shape=jax.ShapeDtypeStruct((rows, cols, channels), BF16),
        in_specs=[smem] + [vmem] * 7,
        scratch_shapes=[pad, cells_scratch],
        compiler_params=params,
        cost_estimate=pl.CostEstimate(flops=10000000, transcendentals=0, bytes_accessed=3000000),
        name="state",
    )(odd, grad_depth, *rows_sent, *cols_sent, cot, dw_kernel)
    value, grad_state = lax.optimization_barrier((value, grad_state))
    other = lax.ppermute(value, "core", [(0, 1), (1, 0)])
    total_cells = cells * lax.axis_size(LON) * lax.axis_size(LAT)
    factor = 1.0 / math.sqrt(total_cells)
    single = jax.ShapeDtypeStruct((1, channels), F32)
    sums = pl.pallas_call(
        functools.partial(unpack_kernel, factor),
        out_shape=(
            jax.ShapeDtypeStruct(dw_kernel.shape, F32),
            single,
            single,
            single,
            jax.ShapeDtypeStruct((channels, hidden), F32),
            jax.ShapeDtypeStruct((1, hidden), F32),
            jax.ShapeDtypeStruct((hidden, channels), F32),
            single,
            single,
        ),
        in_specs=[smem, vmem, vmem],
        scratch_shapes=[pltpu.VMEM((128, LANES), F32)],
        compiler_params=params,
        name="unpack",
    )(core.astype(jnp.int32).reshape(1), value, other)
    sums = [part[0] if part.shape[0] == 1 else part for part in sums]
    return (output[None], grad_state[None], *sums)


def solution(mesh):
    mesh = Mesh(mesh.devices.reshape(tuple(SIZES.values())), EVERY)
    field = P(None, LAT, LON, None)
    in_specs = (field, P(None, LAT, LON), field) + (P(),) * 9
    out_specs = (field, field) + (P(),) * 9
    return jax.shard_map(local, mesh=mesh, in_specs=in_specs, out_specs=out_specs, check_vma=False)
```

```python
import functools
import math

import jax
import jax.numpy as jnp
import numpy as np
from jax import lax
from jax.experimental import pallas as pl
from jax.experimental.pallas import tpu as pltpu
from jax.sharding import Mesh, PartitionSpec as P

LON = ("y_lo", "core")
LAT = ("x", "y_hi", "z")
SIZES = {"y_lo": 4, "core": 2, "x": 4, "y_hi": 2, "z": 8}
EVERY = tuple(SIZES)
BIG_ROWS = 64
CHUNK_ROWS = 72
LANES = 128
VMEM_BYTES = 32 << 20
F32 = jnp.float32
BF16 = jnp.bfloat16


def dot(a, b, ca, cb):
    return lax.dot_general(a, b, (((ca,), (cb,)), ((), ())), preferred_element_type=F32)


def fill_padded(odd_ref, pad_ref, own_ref, near_rows_ref, far_rows_ref, far_cols_ref, near_cols_ref):
    rows, cols, _ = own_ref.shape
    low = rows + 3
    near_at = jnp.where(odd_ref[0] == 1, 0, low)
    far_at = low - near_at
    for t in range(2):
        ln = slice(t * LANES, (t + 1) * LANES)
        pad_ref[t, 3 : 3 + rows, 8 : 8 + cols] = own_ref[:, :, ln].astype(F32)
        pad_ref[t, pl.ds(near_at, 3), 8 : 8 + cols] = near_rows_ref[:, :, ln].astype(F32)
        pad_ref[t, pl.ds(far_at, 3), 8 : 8 + cols] = far_rows_ref[:, :, ln].astype(F32)

    def place(left_ref, right_ref):
        for t in range(2):
            ln = slice(t * LANES, (t + 1) * LANES)
            pad_ref[t, :, 5:8] = left_ref[:, :, ln].astype(F32)
            pad_ref[t, :, 8 + cols : 11 + cols] = right_ref[:, :, ln].astype(F32)

    @pl.when(odd_ref[1] == 0)
    def _():
        place(far_cols_ref, near_cols_ref)

    @pl.when(odd_ref[1] != 0)
    def _():
        place(near_cols_ref, far_cols_ref)


def convolve(pad_ref, k_ref, out_ref, rows, cols, flip):
    blocks = 4
    for t in range(2):
        ln = slice(t * LANES, (t + 1) * LANES)

        def step(n, carry, t=t, ln=ln):
            at = pl.multiple_of(n * 8 * blocks, 8)
            acc = [[jnp.zeros((8, LANES), F32) for _ in range(rows)] for _ in range(blocks)]
            for j in range(7):
                window = [
                    [pad_ref[t, r, pl.ds(at + 8 * b + 5 + j, 8), :] for r in range(rows + 6)] for b in range(blocks)
                ]
                for i in range(7):
                    row, col = (6 - i, 6 - j) if flip else (i, j)
                    weight = k_ref[row, col : col + 1, ln]
                    for b in range(blocks):
                        for p in range(rows):
                            acc[b][p] = acc[b][p] + window[b][p + i] * weight
            for b in range(blocks):
                for p in range(rows):
                    out_ref[t, p, pl.ds(at + 8 * b, 8), :] = acc[b][p]
            return carry

        lax.fori_loop(0, cols // (8 * blocks), step, 0)


def kernel_sums(pad_ref, grad_ref, small_ref, rows, cols):
    for t in range(2):
        for j in range(7):
            acc = [jnp.zeros((8, LANES), F32) for _ in range(7)]
            for b in range(cols // 8):
                window = [pad_ref[t, r, b * 8 + 5 + j : b * 8 + 13 + j, :] for r in range(rows + 6)]
                grad = [grad_ref[t, p, b * 8 : b * 8 + 8, :] for p in range(rows)]
                for i in range(7):
                    part = window[i] * grad[0]
                    for p in range(1, rows):
                        part = part + window[p + i] * grad[p]
                    acc[i] = acc[i] + part
            for i in range(7):
                at = t * 64 + j * 7 + i
                small_ref[at : at + 1, :] = jnp.sum(acc[i], axis=0, keepdims=True)


def write_chunks(chunk_ref, base, part):
    for n in range(part.shape[0] // BIG_ROWS):
        chunk_ref[base + n] = part[n * BIG_ROWS : (n + 1) * BIG_ROWS]


def block_kernel(
    odd_ref, own_ref, near_rows_ref, far_rows_ref, far_cols_ref, near_cols_ref, mask_ref, masked_ref, k_ref, dw_bias_ref,
    gain_ref, bias_ref, w_in_ref, b_in_ref, w_out_hbm_ref, b_out_ref, scale_ref,
    out_ref, grad_ref, chunk_ref, singles_ref,
    pad_ref, depth_ref, w_out_ref, w_out_sem,
):
    rows, cols, channels = own_ref.shape
    cells = rows * cols
    hidden = w_in_ref.shape[1]
    halves = channels // LANES
    w_out_copy = pltpu.make_async_copy(w_out_hbm_ref, w_out_ref, w_out_sem)
    w_out_copy.start()
    fill_padded(odd_ref, pad_ref, own_ref, near_rows_ref, far_rows_ref, far_cols_ref, near_cols_ref)
    convolve(pad_ref, k_ref, depth_ref, rows, cols, False)
    depth = jnp.concatenate([depth_ref[t].reshape(cells, LANES) for t in range(2)], axis=1)
    depth = depth + dw_bias_ref[...]
    center = depth - jnp.mean(depth, axis=-1, keepdims=True)
    inv_std = lax.rsqrt(jnp.mean(center * center, axis=-1, keepdims=True) + 1e-6)
    norm_hat = center * inv_std
    normed = (norm_hat * gain_ref[...] + bias_ref[...]).astype(BF16)
    masked = masked_ref[...].astype(F32)
    grad_branch = (masked * scale_ref[...]).astype(BF16)
    branch = jnp.zeros((cells, channels), F32)
    grad_norm = jnp.zeros((cells, channels), F32)
    root = math.sqrt(2.0 / math.pi)
    w_out_copy.wait()
    b_in_sums = []
    width = channels
    for h in range(hidden // width):
        at = slice(h * width, (h + 1) * width)
        w_in = w_in_ref[:, at]
        w_out = w_out_ref[at, :]
        pre = dot(normed, w_in, 1, 0) + b_in_ref[:, at]
        square = pre * pre
        bent = jnp.tanh(root * pre * (1.0 + 0.044715 * square))
        half = 0.5 * (1.0 + bent)
        act = (pre * half).astype(BF16)
        slope = half + (0.5 * root) * pre * (1.0 - bent * bent) * (1.0 + (3 * 0.044715) * square)
        grad_pre = (dot(grad_branch, w_out, 1, 1) * slope).astype(BF16)
        branch = branch + dot(act, w_out, 1, 0)
        grad_norm = grad_norm + dot(grad_pre, w_in, 1, 1)
        g_in = dot(normed, grad_pre, 0, 0).astype(BF16)
        g_out = dot(act, grad_branch, 0, 0).astype(BF16)
        for t in range(width // LANES):
            base = (h * (width // LANES) + t) * (channels // BIG_ROWS)
            write_chunks(chunk_ref, base, g_in[:, t * LANES : (t + 1) * LANES])
        for t in range(halves):
            base = (hidden * halves + t * hidden + h * width) // BIG_ROWS
            write_chunks(chunk_ref, base, g_out[:, t * LANES : (t + 1) * LANES])
        b_in_sums.append(jnp.sum(grad_pre.astype(F32), axis=0, keepdims=True))
    branch = branch + b_out_ref[...]
    mask = mask_ref[...].astype(F32)
    own = own_ref[...].reshape(cells, channels).astype(F32)
    out_ref[...] = (own + mask * scale_ref[...] * branch).astype(BF16).reshape(rows, cols, channels)
    scaled = grad_norm * gain_ref[...]
    mean_u = jnp.mean(scaled, axis=-1, keepdims=True)
    mean_un = jnp.mean(scaled * norm_hat, axis=-1, keepdims=True)
    grad_depth = (inv_std * (scaled - mean_u - norm_hat * mean_un)).astype(BF16)
    grad_ref[...] = grad_depth.reshape(rows, cols, channels)
    grad_float = grad_depth.astype(F32)
    singles = b_in_sums + [
        jnp.sum(grad_float, axis=0, keepdims=True),
        jnp.sum(grad_norm * norm_hat, axis=0, keepdims=True),
        jnp.sum(grad_norm, axis=0, keepdims=True),
        jnp.sum(grad_branch.astype(F32), axis=0, keepdims=True),
        jnp.sum(masked * branch, axis=0, keepdims=True),
    ]
    for n, single in enumerate(singles):
        singles_ref[n : n + 1, :] = single


def sums_kernel(
    odd_ref, own_ref, near_rows_ref, far_rows_ref, far_cols_ref, near_cols_ref, grad_ref, singles_ref, out_ref,
    pad_ref, grad_float_ref, small_ref,
):
    rows, cols, _ = own_ref.shape
    singles = singles_ref.shape[0]
    fill_padded(odd_ref, pad_ref, own_ref, near_rows_ref, far_rows_ref, far_cols_ref, near_cols_ref)
    for t in range(2):
        ln = slice(t * LANES, (t + 1) * LANES)
        grad_float_ref[t] = grad_ref[:, :, ln].astype(F32)
        small_ref[t * 64 + 49 : t * 64 + 49 + singles, :] = singles_ref[:, ln]
        small_ref[t * 64 + 49 + singles : t * 64 + 64, :] = jnp.zeros((15 - singles, LANES), F32)
    kernel_sums(pad_ref, grad_float_ref, small_ref, rows, cols)
    out_ref[0:16] = small_ref[...].reshape(16, 8, LANES).astype(BF16)
    out_ref[16:] = jnp.zeros((out_ref.shape[0] - 16, 8, LANES), BF16)


def merge_kernel(pair_ref, small_ref, out_ref):
    out_ref[:, 0:BIG_ROWS, :] = (pair_ref[0].astype(F32) + pair_ref[1].astype(F32)).astype(BF16)
    out_ref[:, BIG_ROWS:, :] = small_ref[...]


def state_kernel(
    odd_ref, own_ref, near_rows_ref, far_rows_ref, far_cols_ref, near_cols_ref, cot_ref, k_ref, out_ref, pad_ref, sum_ref
):
    rows, cols, _ = own_ref.shape
    fill_padded(odd_ref, pad_ref, own_ref, near_rows_ref, far_rows_ref, far_cols_ref, near_cols_ref)
    convolve(pad_ref, k_ref, sum_ref, rows, cols, True)
    for t in range(2):
        ln = slice(t * LANES, (t + 1) * LANES)
        out_ref[:, :, ln] = (cot_ref[:, :, ln].astype(F32) + sum_ref[t]).astype(BF16)


def unpack_kernel(
    factor, core_ref, mine_ref, other_ref, k_ref, one_ref, two_ref, three_ref, w_in_ref, b_in_ref, w_out_ref, four_ref,
    five_ref, small_ref,
):
    channels, hidden = w_in_ref.shape

    def rows_of(ref, at, size):
        part = ref[at // BIG_ROWS : (at + size) // BIG_ROWS, 0:BIG_ROWS, :]
        return part.astype(F32).reshape(size, LANES) * factor

    def write(first_ref, second_ref):
        for t in range(hidden // LANES):
            w_in_ref[:, t * LANES : (t + 1) * LANES] = rows_of(first_ref, t * channels, channels)
        for t in range(channels // LANES):
            w_out_ref[:, t * LANES : (t + 1) * LANES] = rows_of(second_ref, t * hidden, hidden)

    @pl.when(core_ref[0] == 0)
    def _():
        write(mine_ref, other_ref)

    @pl.when(core_ref[0] != 0)
    def _():
        write(other_ref, mine_ref)

    small = mine_ref[0:16, BIG_ROWS:, :].astype(F32) + other_ref[0:16, BIG_ROWS:, :].astype(F32)
    small_ref[...] = small.reshape(128, LANES) * factor
    blocks = hidden // channels
    for t in range(2):
        ln = slice(t * LANES, (t + 1) * LANES)
        for j in range(7):
            for i in range(7):
                at = t * 64 + j * 7 + i
                k_ref[i, j : j + 1, ln] = small_ref[at : at + 1, :]
        at = t * 64 + 49
        for n in range(blocks):
            part = slice(n * channels + t * LANES, n * channels + (t + 1) * LANES)
            b_in_ref[:, part] = small_ref[at + n : at + n + 1, :]
        for n, ref in enumerate((one_ref, two_ref, three_ref, four_ref, five_ref)):
            ref[:, ln] = small_ref[at + blocks + n : at + blocks + n + 1, :]


def groups_along(first_core, second_core):
    index = np.arange(math.prod(SIZES.values())).reshape(tuple(SIZES.values()))
    groups = []
    for core, axes in enumerate((first_core, second_core)):
        mine = index.take(core, axis=EVERY.index("core"))
        names = [name for name in EVERY if name != "core"]
        order = [name for name in names if name not in axes] + list(axes)
        size = math.prod(SIZES[name] for name in axes)
        groups += mine.transpose([names.index(name) for name in order]).reshape(-1, size).tolist()
    return groups


PLANE = groups_along(("x", "z"), ("x", "y_hi", "y_lo"))
COLUMN = groups_along(("y_hi", "y_lo"), ("z",))


def exchange(value, groups):
    return lax.all_to_all(value, EVERY, 0, 0, axis_index_groups=groups)


def swaps(axis, wrap):
    size = lax.axis_size(axis)
    near = [(i, i ^ 1) for i in range(size)]
    far = []
    for i in range(1, size if wrap else size - 1, 2):
        far += [(i, (i + 1) % size), ((i + 1) % size, i)]
    return near, far


def swap_rows(field, odd):
    rows = field.shape[0]
    near, far = swaps(LAT, False)
    first, last = field[:3], field[rows - 3 :]
    far_rows = lax.ppermute(jnp.where(odd, last, first), LAT, far)
    near_rows = lax.ppermute(jnp.where(odd, first, last), LAT, near)
    return near_rows, far_rows


def swap_cols(field, near_rows, far_rows, odd_lat, odd_lon):
    cols = field.shape[1]
    near, far = swaps(LON, True)

    def strip(at):
        part = slice(at, at + 3)
        before = jnp.where(odd_lat, near_rows[:, part], far_rows[:, part])
        after = jnp.where(odd_lat, far_rows[:, part], near_rows[:, part])
        return jnp.concatenate([before, field[:, part], after], axis=0)

    first, last = strip(0), strip(cols - 3)
    far_cols = lax.ppermute(jnp.where(odd_lon, last, first), LON, far)
    near_cols = lax.ppermute(jnp.where(odd_lon, first, last), LON, near)
    return far_cols, near_cols


def local(
    ocean_state, land_sea, cotangent, dw_kernel, dw_bias, ln_gain, ln_bias, w_in, b_in, w_out, b_out, layer_scale
):
    _, rows, cols, channels = ocean_state.shape
    cells = rows * cols
    hidden = w_in.shape[1]
    plane, column = len(PLANE[0]), len(COLUMN[0])
    core = lax.axis_index("core")
    own = ocean_state[0]
    cot = cotangent[0]
    odd_lat = lax.axis_index("z") & 1
    odd = jnp.stack([odd_lat, core]).astype(jnp.int32)
    odd_lat, odd_lon = odd_lat == 1, core == 1
    near_rows, far_rows = swap_rows(own, odd_lat)
    far_cols, near_cols = swap_cols(own, near_rows, far_rows, odd_lat, odd_lon)
    mask = jnp.broadcast_to(land_sea[0].astype(BF16)[..., None], cot.shape)
    masked = mask * cot
    pad = pltpu.VMEM((2, rows + 6, cols + 16, LANES), F32)
    cells_scratch = pltpu.VMEM((2, rows, cols, LANES), F32)
    smem, vmem = pl.BlockSpec(memory_space=pltpu.SMEM), pl.BlockSpec(memory_space=pltpu.VMEM)
    params = pltpu.CompilerParams(vmem_limit_bytes=VMEM_BYTES)
    blocks = hidden // channels
    output, grad_depth, chunks, singles = pl.pallas_call(
        block_kernel,
        out_shape=(
            jax.ShapeDtypeStruct((rows, cols, channels), BF16),
            jax.ShapeDtypeStruct((rows, cols, channels), BF16),
            jax.ShapeDtypeStruct((2 * plane, BIG_ROWS, LANES), BF16),
            jax.ShapeDtypeStruct((blocks + 5, channels), F32),
        ),
        in_specs=[smem] + [vmem] * 13 + [pl.BlockSpec(memory_space=pltpu.HBM)] + [vmem] * 2,
        scratch_shapes=[
            pad,
            cells_scratch,
            pltpu.VMEM(w_out.shape, BF16),
            pltpu.SemaphoreType.DMA,
        ],
        compiler_params=params,
        cost_estimate=pl.CostEstimate(flops=1300000000, transcendentals=400000, bytes_accessed=6000000),
        name="block",
    )(
        odd, own, near_rows, far_rows, far_cols, near_cols, mask.reshape(cells, channels), masked.reshape(cells, channels), dw_kernel,
        dw_bias[None], ln_gain[None], ln_bias[None], w_in, b_in[None], pltpu.with_memory_space_constraint(w_out, pltpu.HBM), b_out[None], layer_scale[None],
    )
    rows_sent = swap_rows(grad_depth, odd_lat)
    small = pl.pallas_call(
        sums_kernel,
        out_shape=jax.ShapeDtypeStruct((plane, CHUNK_ROWS - BIG_ROWS, LANES), BF16),
        in_specs=[smem] + [vmem] * 7,
        scratch_shapes=[pad, cells_scratch, pltpu.VMEM((128, LANES), F32)],
        compiler_params=params,
        cost_estimate=pl.CostEstimate(flops=10000000, transcendentals=0, bytes_accessed=3000000),
        name="sums",
    )(odd, own, near_rows, far_rows, far_cols, near_cols, grad_depth, singles)
    pair = lax.all_to_all(chunks.reshape(2, plane, BIG_ROWS, LANES), "core", 0, 0)
    pair, small = lax.optimization_barrier((pair, small))
    value = pl.pallas_call(
        merge_kernel,
        out_shape=jax.ShapeDtypeStruct((plane, CHUNK_ROWS, LANES), BF16),
        compiler_params=params,
        cost_estimate=pl.CostEstimate(flops=300000, transcendentals=0, bytes_accessed=2000000),
        name="merge",
    )(pair, small)
    value = exchange(value, PLANE)
    value = jnp.sum(value.astype(F32), axis=0).astype(BF16)
    value, rows_sent = lax.optimization_barrier((value, rows_sent))
    value = exchange(jnp.broadcast_to(value[None], (column,) + value.shape), COLUMN)
    value = jnp.sum(value.astype(F32), axis=0).astype(BF16)
    value = exchange(jnp.broadcast_to(value[None], (plane,) + value.shape), PLANE)
    cols_sent = swap_cols(grad_depth, *rows_sent, odd_lat, odd_lon)
    grad_state = pl.pallas_call(
        state_kernel,
        out_shape=jax.ShapeDtypeStruct((rows, cols, channels), BF16),
        in_specs=[smem] + [vmem] * 7,
        scratch_shapes=[pad, cells_scratch],
        compiler_params=params,
        cost_estimate=pl.CostEstimate(flops=10000000, transcendentals=0, bytes_accessed=3000000),
        name="state",
    )(odd, grad_depth, *rows_sent, *cols_sent, cot, dw_kernel)
    value, grad_state = lax.optimization_barrier((value, grad_state))
    other = lax.ppermute(value, "core", [(0, 1), (1, 0)])
    total_cells = cells * lax.axis_size(LON) * lax.axis_size(LAT)
    factor = 1.0 / math.sqrt(total_cells)
    single = jax.ShapeDtypeStruct((1, channels), F32)
    sums = pl.pallas_call(
        functools.partial(unpack_kernel, factor),
        out_shape=(
            jax.ShapeDtypeStruct(dw_kernel.shape, F32),
            single,
            single,
            single,
            jax.ShapeDtypeStruct((channels, hidden), F32),
            jax.ShapeDtypeStruct((1, hidden), F32),
            jax.ShapeDtypeStruct((hidden, channels), F32),
            single,
            single,
        ),
        in_specs=[smem, vmem, vmem],
        scratch_shapes=[pltpu.VMEM((128, LANES), F32)],
        compiler_params=params,
        name="unpack",
    )(core.astype(jnp.int32).reshape(1), value, other)
    sums = [part[0] if part.shape[0] == 1 else part for part in sums]
    return (output[None], grad_state[None], *sums)


def solution(mesh):
    mesh = Mesh(mesh.devices.reshape(tuple(SIZES.values())), EVERY)
    field = P(None, LAT, LON, None)
    in_specs = (field, P(None, LAT, LON), field) + (P(),) * 9
    out_specs = (field, field) + (P(),) * 9
    return jax.shard_map(local, mesh=mesh, in_specs=in_specs, out_specs=out_specs, check_vma=False)
```
